32 devices in a mesh: dp: 8 (over z, x), tensor: 4 (over y, core).
Axes of the slice: x: 2, y: 2, z: 4, core: 2. Of those that a mesh axis runs over, the one named last changes fastest.
Arguments:
- tokens: bfloat16 [3072, 1024], P('dp'), may hold values from -6 to 6
- segment_ids: int32 [8, 384], P('dp'), may hold values from 0 to 5, never falling along the last dimension, each value on 1 to 192 neighbouring positions
- cotangent: bfloat16 [3072, 1024], P('dp'), may hold values from -6 to 6
- norm1_gain: float32 [1024], replicated, may hold values from 0.5 to 1.5
- norm1_shift: float32 [1024], replicated, may hold values from -3 to 3
- w_qkv: bfloat16 [1024, 3072], P(None, 'tensor'), may hold values from -0.1875 to 0.1875
- b_qkv: float32 [3072], P('tensor'), may hold values from -9 to 9
- w_dense: bfloat16 [1024, 1024], P('tensor'), may hold values from -0.75 to 0.75
- b_dense: float32 [1024], replicated, may hold values from -3 to 3
- norm2_gain: float32 [1024], replicated, may hold values from 0.5 to 1.5
- norm2_shift: float32 [1024], replicated, may hold values from -3 to 3
- w_up: bfloat16 [1024, 4096], P(None, 'tensor'), may hold values from -0.1875 to 0.1875
- b_up: float32 [4096], P('tensor'), may hold values from -3 to 3
- w_down: bfloat16 [4096, 1024], P('tensor'), may hold values from -0.09375 to 0.09375
- b_down: float32 [1024], replicated, may hold values from -3 to 3
Outputs:
- output: bfloat16 [3072, 1024], P('dp')
- grad_input: float32 [3072, 1024], P('dp')
- grad_norm1_gain: float32 [1024], P('dp')
- grad_norm1_shift: float32 [1024], P('dp')
- grad_w_qkv: float32 [1024, 3072], P('dp', 'tensor')
- grad_b_qkv: float32 [3072], P(('tensor', 'dp'))
- grad_w_dense: float32 [1024, 1024], P('tensor', 'dp')
- grad_b_dense: float32 [1024], P('dp')
- grad_norm2_gain: float32 [1024], P('dp')
- grad_norm2_shift: float32 [1024], P('dp')
- grad_w_up: float32 [1024, 4096], P('dp', 'tensor')
- grad_b_up: float32 [4096], P(('tensor', 'dp'))
- grad_w_down: float32 [4096, 1024], P('tensor', 'dp')
- grad_b_down: float32 [1024], P('dp')
The draws below stay inside these ranges and needn't reach their ends.
Inputs may be any that keep to these rules, and one draw needn't show every extreme that they name: `segment_ids`: in each row, ids never fall; each of the 6 sequences has 1 to 192 tokens and one has exactly 192.
All inputs are finite; a program needn't handle non-finite values.
Results may differ from the reference program's by a relative error of at most 0.019.
The reference program's roundings to bfloat16 on the way count: a program that leaves them out, or rounds other values in their place, can miss the bound.
Values sent between devices are 32-bit elements; how exact they have to be, the bound alone decides.
A program may use at most 128 MiB of HBM per device.

```python
import math
import jax
import jax.numpy as jnp
import numpy as np
from jax import lax

D = 1024
H = 16
HD = 64
FF = 4096
TOK_DEV = 384
SEQS = 6
SEG_MAX = 192
TOKENS = 3072
N_DP = 8


def draw_b_qkv(key, part):
    drawn_key, sign_key, spread_key, offset_key = jax.random.split(key, 4)
    drawn_part = jnp.clip(0.5 * jax.random.normal(drawn_key, (H, 3, HD), jnp.float32), -1.5, 1.5)
    levels = jnp.array([0.0, 120.0, 0.0, 260.0], jnp.float32)
    spread = jax.random.uniform(spread_key, (H, HD), jnp.float32, 0.8, 1.2)
    offset = jax.random.randint(offset_key, (), 0, 4)
    strength = jnp.take(levels, (jnp.arange(H) + offset) % 4)
    signs = jnp.where(jax.random.bernoulli(sign_key, 0.5, (H, HD)), 1.0, -1.0)
    aligned = signs * spread * jnp.sqrt(strength / 8.0)[:, None]
    zeros_part = jnp.zeros((H, HD), jnp.float32)
    boost = jnp.stack([aligned, aligned, zeros_part], axis=1)
    return (drawn_part + boost).reshape(3 * D).astype(jnp.float32)


def spiked(values, rng, source, target, blocks, factor):
    def block_of(position):
        return (jnp.arange(values.shape[position]) // (values.shape[position] // blocks)).reshape((-1,) + (1,) * (values.ndim - 1 - position))

    first = jax.random.permutation(rng, blocks)[block_of(target)]
    other_side = (block_of(target) + blocks // 2) % blocks
    return jnp.where((block_of(source) == first) | (block_of(source) == other_side), factor * values, values)


def steps_of(rng, extent, cuts, smallest, largest):
    level = 1.0
    for dim, parts in cuts:
        draws = jax.random.uniform(jax.random.fold_in(jax.random.fold_in(rng, 6), dim), (parts,), jnp.float32, smallest / len(cuts), largest / len(cuts))
        level = level * jnp.repeat(jnp.exp(draws), extent[dim] // parts).reshape((-1,) + (1,) * (len(extent) - 1 - dim))
    return level


def profile(count, total, limit, slope):
    portions = [(1 << 20) // math.isqrt(grade ** slope) + 1 for grade in range(2, count + 1)]
    surplus, given = total - limit - (count - 1), [1] * (count - 1)
    while surplus > 0:
        candidates = [i for i in range(count - 1) if given[i] < limit]
        whole, remaining = sum([portions[i] for i in candidates]), surplus
        for i in candidates:
            more = min(limit - given[i], max(1, remaining * portions[i] // whole), surplus)
            given[i] = given[i] + more
            surplus = surplus - more
    return np.array([limit] + given)


def ragged(own_key, count, total, bound, slope):
    if count == 2:
        one = jax.random.randint(own_key, (), max(1, total - bound), min(bound, total - 1) + 1)
        return jnp.stack([one, total - one])
    sizes = jnp.asarray(profile(count, total, bound, slope), jnp.int32)
    pairs = (count - 1) // 2
    giver, sink = sizes[1:1 + 2 * pairs:2], sizes[2:2 + 2 * pairs:2]
    slack = jnp.minimum(giver - 1, bound - sink)
    shifted = jax.random.randint(jax.random.fold_in(own_key, 1), (pairs,), 0, 1 << 20) % (slack + 1)
    sizes = sizes.at[1:1 + 2 * pairs:2].set(giver - shifted).at[2:2 + 2 * pairs:2].set(sink + shifted)
    return sizes[jax.random.permutation(jax.random.fold_in(own_key, 2), count)]


def gaussian(rng, extent, scale, most, cuts=(), kind=jnp.bfloat16):
    level = steps_of(rng, extent, cuts, -0.22, 0.18) if cuts else 1.0
    values = jax.random.normal(rng, extent, jnp.float32) * scale * level
    return jnp.minimum(jnp.maximum(values, -most), most).astype(kind)


def noise_with(rng, shape, scale, bound, cuts, heavy, held_as=jnp.bfloat16):
    values = scale * jax.random.normal(rng, shape, jnp.float32)
    if cuts:
        values = values * steps_of(rng, shape, cuts, -0.22, 0.18)
    return jnp.clip(spiked(values, jax.random.fold_in(rng, 3), *heavy), -bound, bound).astype(held_as)


def setup_inputs(seed: int = 0) -> dict:
    streams_of = jax.random.split(jax.random.key(seed), 16)
    return {
        "tokens": noise_with(streams_of[0], (TOKENS, D), 1.0, 6.0, ((0, 8),), (0, 1, 8, 2.0)),
        "segment_ids": jax.vmap(lambda own: jnp.searchsorted(jnp.cumsum(ragged(own, SEQS, TOK_DEV, SEG_MAX, 2)), jnp.arange(TOK_DEV), side="right"))(jax.random.split(streams_of[1], N_DP)).reshape((N_DP, TOK_DEV)).astype(jnp.int32),
        "cotangent": noise_with(streams_of[2], (TOKENS, D), 1.0, 6.0, ((0, 8),), (0, 1, 8, 2.0)),
        "norm1_gain": jnp.clip(jax.random.uniform(streams_of[3], (D,), jnp.float32, 0.5, 1.5), 0.5, 1.5),
        "norm1_shift": gaussian(streams_of[4], (D,), 0.5, 3.0, (), jnp.float32),
        "w_qkv": gaussian(streams_of[5], (D, 3 * D), D ** -0.5, 0.1875, ((1, 4),)),
        "b_qkv": draw_b_qkv(jax.random.fold_in(streams_of[15], 71), 0),
        "w_dense": gaussian(streams_of[7], (D, D), HD ** -0.5, 0.75, ((0, 4),)),
        "b_dense": gaussian(streams_of[8], (D,), 0.5, 3.0, (), jnp.float32),
        "norm2_gain": jnp.clip(jax.random.uniform(streams_of[9], (D,), jnp.float32, 0.5, 1.5), 0.5, 1.5),
        "norm2_shift": gaussian(streams_of[10], (D,), 0.5, 3.0, (), jnp.float32),
        "w_up": gaussian(streams_of[11], (D, FF), D ** -0.5, 0.1875, ((1, 4),)),
        "b_up": gaussian(streams_of[12], (FF,), 0.5, 3.0, ((0, 4),), jnp.float32),
        "w_down": gaussian(streams_of[13], (FF, D), FF ** -0.5, 0.09375, ((0, 4),)),
        "b_down": gaussian(streams_of[14], (D,), 0.5, 3.0, (), jnp.float32),
    }


EPSILON = 1e-05
GELU_COEF = math.sqrt(2.0 / math.pi)

def layer_norm(values, gain, shift):
    average = lax.optimization_barrier(jnp.mean(values, axis=-1, keepdims=True))
    centered = values - average
    variance = lax.optimization_barrier(jnp.mean(centered * centered, axis=-1, keepdims=True))
    inverse = lax.rsqrt(variance + EPSILON)
    normed = centered * inverse
    return (normed * gain + shift, normed, inverse)

def norm_backward(upstream, normed, inverse, gain):
    scaled = upstream * gain
    return inverse * (scaled - lax.optimization_barrier(jnp.mean(scaled, axis=-1, keepdims=True)) - normed * lax.optimization_barrier(jnp.mean(scaled * normed, axis=-1, keepdims=True)))

def gelu_pair(inputs):
    tangent = jnp.tanh(GELU_COEF * (inputs + 0.044715 * inputs * inputs * inputs))
    result = 0.5 * inputs * (1.0 + tangent)
    derivative = 0.5 * (1.0 + tangent) + 0.5 * inputs * (1.0 - tangent * tangent) * GELU_COEF * (1.0 + 3.0 * 0.044715 * inputs * inputs)
    return (result, derivative)

def shard_pass(tokens, segments, cotangent, norm1_gain, norm1_shift, w_qkv, b_qkv, w_dense, b_dense, norm2_gain, norm2_shift, w_up, b_up, w_down, b_down):
    row_count = tokens.shape[0]
    scaling = 1.0 / math.sqrt(HD)
    inputs = tokens.astype(jnp.float32)
    first_out, normed1, inverse1 = layer_norm(inputs, norm1_gain, norm1_shift)
    first_in = first_out.astype(jnp.bfloat16)
    joined = (jnp.dot(first_in, w_qkv, preferred_element_type=jnp.float32) + b_qkv).astype(jnp.bfloat16)
    joined = joined.reshape(row_count, H, 3, HD)
    queries = joined[:, :, 0].astype(jnp.float32)
    key_vecs = joined[:, :, 1].astype(jnp.float32)
    val_vecs = joined[:, :, 2].astype(jnp.float32)
    slopes = 2.0 ** (-8.0 * (jnp.arange(H) + 1).astype(jnp.float32) / H)
    places = jnp.arange(row_count)
    offset = (places[None, :] - places[:, None]).astype(jnp.float32)
    allowed = (segments[:, None] == segments[None, :]) & (places[None, :] <= places[:, None])
    raw_scores = jnp.einsum('ihe,jhe->hij', queries, key_vecs)
    scores = jnp.where(allowed[None], raw_scores * scaling + slopes[:, None, None] * offset[None], -1e+30)
    highest = lax.optimization_barrier(jnp.max(scores, axis=-1, keepdims=True))
    log_total = highest + jnp.log(lax.optimization_barrier(jnp.sum(jnp.exp(scores - highest), axis=-1, keepdims=True)))
    attn_probs = jnp.exp(scores - log_total)
    probs_b = attn_probs.astype(jnp.bfloat16).astype(jnp.float32)
    context = jnp.einsum('hij,jhe->ihe', probs_b, val_vecs).astype(jnp.bfloat16).reshape(row_count, D)
    hidden = inputs + jnp.dot(context, w_dense, preferred_element_type=jnp.float32) + b_dense
    second_out, normed2, inverse2 = layer_norm(hidden, norm2_gain, norm2_shift)
    second_in = second_out.astype(jnp.bfloat16)
    upward = jnp.dot(second_in, w_up, preferred_element_type=jnp.float32) + b_up
    activated, gelu_slope = gelu_pair(upward)
    activated_b = activated.astype(jnp.bfloat16)
    output = (hidden + jnp.dot(activated_b, w_down, preferred_element_type=jnp.float32) + b_down).astype(jnp.bfloat16)
    grad_out = cotangent.astype(jnp.float32)
    grad_w_down = jnp.dot(activated_b.T, cotangent, preferred_element_type=jnp.float32)
    grad_b_down = lax.optimization_barrier(jnp.sum(grad_out, axis=0))
    grad_up = jnp.dot(cotangent, w_down.T, preferred_element_type=jnp.float32) * gelu_slope
    grad_up_b = grad_up.astype(jnp.bfloat16)
    grad_w_up = jnp.dot(second_in.T, grad_up_b, preferred_element_type=jnp.float32)
    grad_b_up = lax.optimization_barrier(jnp.sum(grad_up, axis=0))
    grad_norm2 = jnp.dot(grad_up_b, w_up.T, preferred_element_type=jnp.float32)
    grad_gain2 = lax.optimization_barrier(jnp.sum(grad_norm2 * normed2, axis=0))
    grad_shift2 = lax.optimization_barrier(jnp.sum(grad_norm2, axis=0))
    grad_hidden = grad_out + norm_backward(grad_norm2, normed2, inverse2, norm2_gain)
    grad_hidden_b = grad_hidden.astype(jnp.bfloat16)
    grad_w_dense = jnp.dot(context.T, grad_hidden_b, preferred_element_type=jnp.float32)
    grad_b_dense = lax.optimization_barrier(jnp.sum(grad_hidden, axis=0))
    grad_context = jnp.dot(grad_hidden_b, w_dense.T, preferred_element_type=jnp.float32).astype(jnp.bfloat16)
    grad_context = grad_context.reshape(row_count, H, HD).astype(jnp.float32)
    grad_vals = jnp.einsum('hij,ihe->jhe', probs_b, grad_context)
    grad_probs = jnp.einsum('ihe,jhe->hij', grad_context, val_vecs)
    row_inner = lax.optimization_barrier(jnp.sum(attn_probs * grad_probs, axis=-1, keepdims=True))
    grad_scores = (attn_probs * (grad_probs - row_inner)).astype(jnp.bfloat16).astype(jnp.float32)
    grad_queries = jnp.einsum('hij,jhe->ihe', grad_scores, key_vecs) * scaling
    grad_keys = jnp.einsum('hij,ihe->jhe', grad_scores, queries) * scaling
    grad_joined = jnp.stack([grad_queries, grad_keys, grad_vals], axis=2).reshape(row_count, 3 * D)
    grad_joined_b = grad_joined.astype(jnp.bfloat16)
    grad_w_qkv = jnp.dot(first_in.T, grad_joined_b, preferred_element_type=jnp.float32)
    grad_b_qkv = lax.optimization_barrier(jnp.sum(grad_joined, axis=0))
    grad_norm1 = jnp.dot(grad_joined_b, w_qkv.T, preferred_element_type=jnp.float32)
    grad_gain1 = lax.optimization_barrier(jnp.sum(grad_norm1 * normed1, axis=0))
    grad_shift1 = lax.optimization_barrier(jnp.sum(grad_norm1, axis=0))
    grad_input = grad_hidden + norm_backward(grad_norm1, normed1, inverse1, norm1_gain)
    grads = (grad_gain1, grad_shift1, grad_w_qkv, grad_b_qkv, grad_w_dense, grad_b_dense, grad_gain2, grad_shift2, grad_w_up, grad_b_up, grad_w_down, grad_b_down)
    return (output, grad_input, grads)

def reference(tokens, segment_ids, cotangent, norm1_gain, norm1_shift, w_qkv, b_qkv, w_dense, b_dense, norm2_gain, norm2_shift, w_up, b_up, w_down, b_down):
    shards = segment_ids.shape[0]
    token_blocks = tokens.reshape(shards, TOK_DEV, D)
    cot_blocks = cotangent.reshape(shards, TOK_DEV, D)
    initial = (jnp.zeros((D,), jnp.float32), jnp.zeros((D,), jnp.float32), jnp.zeros((D, 3 * D), jnp.float32), jnp.zeros((3 * D,), jnp.float32), jnp.zeros((D, D), jnp.float32), jnp.zeros((D,), jnp.float32), jnp.zeros((D,), jnp.float32), jnp.zeros((D,), jnp.float32), jnp.zeros((D, FF), jnp.float32), jnp.zeros((FF,), jnp.float32), jnp.zeros((FF, D), jnp.float32), jnp.zeros((D,), jnp.float32))

    def step_fn(carry, pieces):
        block, segments, cot_block = pieces
        output, grad_input, grads = shard_pass(block, segments, cot_block, norm1_gain, norm1_shift, w_qkv, b_qkv, w_dense, b_dense, norm2_gain, norm2_shift, w_up, b_up, w_down, b_down)
        carry = jax.tree.map(lambda left, right: left + right, carry, grads)
        return (carry, (output, grad_input))
    totals, (outputs, grad_inputs) = lax.scan(step_fn, initial, (token_blocks, segment_ids, cot_blocks))
    return (outputs.reshape(shards * TOK_DEV, D), grad_inputs.reshape(shards * TOK_DEV, D)) + tuple(totals)
```

```python
import functools
import math
from types import SimpleNamespace

import jax
import jax.numpy as jnp
from jax import lax
from jax.experimental import pallas as pl
from jax.experimental.pallas import tpu as pltpu
from jax.sharding import PartitionSpec as P

H = 16
HD = 64


EPSILON = 1e-05
GELU_COEF = math.sqrt(2.0 / math.pi)


def layer_norm(values, gain, shift):
    average = jnp.mean(values, axis=-1, keepdims=True)
    centered = values - average
    variance = jnp.mean(centered * centered, axis=-1, keepdims=True)
    inverse = lax.rsqrt(variance + EPSILON)
    normed = centered * inverse
    return (normed * gain + shift, normed, inverse)


def norm_backward(upstream, normed, inverse, gain):
    scaled = upstream * gain
    return inverse * (
        scaled
        - jnp.mean(scaled, axis=-1, keepdims=True)
        - normed * jnp.mean(scaled * normed, axis=-1, keepdims=True)
    )


def gelu_pair(inputs):
    tangent = jnp.tanh(GELU_COEF * (inputs + 0.044715 * inputs * inputs * inputs))
    result = 0.5 * inputs * (1.0 + tangent)
    derivative = 0.5 * (1.0 + tangent) + 0.5 * inputs * (1.0 - tangent * tangent) * GELU_COEF * (
        1.0 + 3.0 * 0.044715 * inputs * inputs
    )
    return (result, derivative)


def head_scores(queries, key_vecs, slopes, offset, allowed, scaling):
    raw_scores = jnp.einsum("ihe,jhe->hij", queries, key_vecs, preferred_element_type=jnp.float32)
    return jnp.where(
        allowed[None], raw_scores * scaling + slopes[:, None, None] * offset[None], -1e30
    )

CHUNKS = 4
MESH = pl.DeviceIdType.MESH
MIB = 1024 * 1024


def scatter(grads, kinds):
    return [
        lax.psum_scatter(g, "dp", scatter_dimension=0 if k == "rows" else 1, tiled=True)
        for g, k in zip(grads, kinds)
    ]


def scatter_vectors(vectors, n_dp):
    widths = [v.shape[0] // n_dp for v in vectors]
    widest = -(-max(widths) // 128) * 128
    table = jnp.stack(
        [jnp.pad(v.reshape(n_dp, -1), ((0, 0), (0, widest - w))) for v, w in zip(vectors, widths)],
        axis=1,
    ).reshape(n_dp * len(vectors), widest)
    (mine,) = scatter([table], ["rows"])
    return [mine[i, :w] for i, w in enumerate(widths)]


def local(
    sizes,
    tokens,
    segment_ids,
    cotangent,
    norm1_gain,
    norm1_shift,
    w_qkv,
    b_qkv,
    w_dense,
    b_dense,
    norm2_gain,
    norm2_shift,
    w_up,
    b_up,
    w_down,
    b_down,
):
    segments = segment_ids[0]
    row_count = tokens.shape[0]
    heads_here = w_qkv.shape[1] // (3 * HD)
    head_start = lax.axis_index("tensor") * heads_here
    scaling = 1.0 / math.sqrt(HD)
    slopes = 2.0 ** (-8.0 * (head_start + jnp.arange(heads_here) + 1).astype(jnp.float32) / H)
    places = jnp.arange(row_count)
    offset = (places[None, :] - places[:, None]).astype(jnp.float32)
    allowed = (segments[:, None] == segments[None, :]) & (places[None, :] <= places[:, None])
    inputs = tokens.astype(jnp.float32)
    first_out, normed1, inverse1 = layer_norm(inputs, norm1_gain, norm1_shift)
    first_in = first_out.astype(jnp.bfloat16)
    joined = (jnp.dot(first_in, w_qkv, preferred_element_type=jnp.float32) + b_qkv).astype(
        jnp.bfloat16
    )
    joined = joined.reshape(row_count, heads_here, 3, HD)
    queries = joined[:, :, 0]
    key_vecs = joined[:, :, 1]
    val_vecs = joined[:, :, 2]
    scores = head_scores(queries, key_vecs, slopes, offset, allowed, scaling)
    highest = jnp.max(scores, axis=-1, keepdims=True)
    log_total = highest + jnp.log(jnp.sum(jnp.exp(scores - highest), axis=-1, keepdims=True))
    probs = jnp.exp(scores - log_total)
    probs_b = probs.astype(jnp.bfloat16)
    context = jnp.einsum(
        "hij,jhe->ihe", probs_b, val_vecs, preferred_element_type=jnp.float32
    ).astype(jnp.bfloat16)
    context = context.reshape(row_count, heads_here * HD)
    attended = lax.psum(jnp.dot(context, w_dense, preferred_element_type=jnp.float32), "tensor")
    hidden = inputs + attended + b_dense
    second_out, normed2, inverse2 = layer_norm(hidden, norm2_gain, norm2_shift)
    second_in = second_out.astype(jnp.bfloat16)
    upward = jnp.dot(second_in, w_up, preferred_element_type=jnp.float32) + b_up
    activated, gelu_slope = gelu_pair(upward)
    activated_b = activated.astype(jnp.bfloat16)
    mixed = jnp.dot(activated_b, w_down, preferred_element_type=jnp.float32)
    grad_out = cotangent.astype(jnp.float32)
    grad_w_down = jnp.dot(activated_b.T, cotangent, preferred_element_type=jnp.float32)
    grad_b_down = jnp.sum(grad_out, axis=0)
    grad_up = jnp.dot(cotangent, w_down.T, preferred_element_type=jnp.float32) * gelu_slope
    grad_up_b = grad_up.astype(jnp.bfloat16)
    grad_w_up = jnp.dot(second_in.T, grad_up_b, preferred_element_type=jnp.float32)
    grad_b_up = jnp.sum(grad_up, axis=0)
    grad_norm2 = jnp.dot(grad_up_b, w_up.T, preferred_element_type=jnp.float32)
    grad_norm2 = lax.psum(grad_norm2, "tensor")
    mixed = lax.psum(mixed, "tensor")
    grad_hidden = grad_out + norm_backward(grad_norm2, normed2, inverse2, norm2_gain)
    grad_hidden_b = grad_hidden.astype(jnp.bfloat16)
    grad_w_dense = jnp.dot(context.T, grad_hidden_b, preferred_element_type=jnp.float32)
    grad_context = jnp.dot(grad_hidden_b, w_dense.T, preferred_element_type=jnp.float32).astype(
        jnp.bfloat16
    )
    grad_context = grad_context.reshape(row_count, heads_here, HD)
    scores_again = head_scores(queries, key_vecs, slopes, offset, allowed, scaling)
    probs_again = jnp.exp(scores_again - log_total)
    probs_again_b = probs_again.astype(jnp.bfloat16)
    grad_vals = jnp.einsum(
        "hij,ihe->jhe", probs_again_b, grad_context, preferred_element_type=jnp.float32
    )
    grad_probs = jnp.einsum(
        "ihe,jhe->hij", grad_context, val_vecs, preferred_element_type=jnp.float32
    )
    row_inner = jnp.sum(probs_again * grad_probs, axis=-1, keepdims=True)
    grad_scores = (probs_again * (grad_probs - row_inner)).astype(jnp.bfloat16)
    grad_queries = (
        jnp.einsum("hij,jhe->ihe", grad_scores, key_vecs, preferred_element_type=jnp.float32)
        * scaling
    )
    grad_keys = (
        jnp.einsum("hij,ihe->jhe", grad_scores, queries, preferred_element_type=jnp.float32)
        * scaling
    )
    grad_joined = jnp.stack([grad_queries, grad_keys, grad_vals], axis=2).reshape(
        row_count, 3 * heads_here * HD
    )
    grad_joined_b = grad_joined.astype(jnp.bfloat16)
    grad_w_qkv = jnp.dot(first_in.T, grad_joined_b, preferred_element_type=jnp.float32)
    grad_norm1 = jnp.dot(grad_joined_b, w_qkv.T, preferred_element_type=jnp.float32)
    grad_norm1 = lax.psum(grad_norm1, "tensor")
    grad_w_up, grad_w_down, grad_w_qkv, grad_w_dense = scatter(
        [grad_w_up, grad_w_down, grad_w_qkv, grad_w_dense],
        ["rows", "columns", "rows", "columns"],
    )
    output = (hidden + mixed + b_down).astype(jnp.bfloat16)
    grad_gain2 = jnp.sum(grad_norm2 * normed2, axis=0)
    grad_shift2 = jnp.sum(grad_norm2, axis=0)
    grad_b_dense = jnp.sum(grad_hidden, axis=0)
    grad_b_qkv = jnp.sum(grad_joined, axis=0)
    grad_gain1 = jnp.sum(grad_norm1 * normed1, axis=0)
    grad_shift1 = jnp.sum(grad_norm1, axis=0)
    grad_input = grad_hidden + norm_backward(grad_norm1, normed1, inverse1, norm1_gain)
    vectors = scatter_vectors(
        [
            grad_gain1,
            grad_shift1,
            grad_b_qkv,
            grad_b_dense,
            grad_gain2,
            grad_shift2,
            grad_b_up,
            grad_b_down,
        ],
        sizes[0],
    )
    gain1, shift1, b_qkv_part, b_dense_part, gain2, shift2, b_up_part, b_down_part = vectors
    return (
        output,
        grad_input,
        gain1,
        shift1,
        grad_w_qkv,
        b_qkv_part,
        grad_w_dense,
        b_dense_part,
        gain2,
        shift2,
        grad_w_up,
        b_up_part,
        grad_w_down,
        b_down_part,
    )


W = 256
B = 128
SUMS = 4
ATT, GN2, MIX, GN1 = range(SUMS)
COT, FI, SI, GH = range(4)
GAIN1, SHIFT1, BQKV, BDENSE, GAIN2, SHIFT2, BUP, BDOWN = range(8)
N_TALL = 5
ORDER = (3, 0, 2, 1)
f32 = jnp.float32
bf16 = jnp.bfloat16


def contract(left, right, left_axis, right_axis):
    return lax.dot_general(
        left, right, (((left_axis,), (right_axis,)), ((), ())), preferred_element_type=f32
    )


def loop(count, body):
    def step(i, carry):
        body(i)
        return carry

    lax.fori_loop(0, count, step, 0)


def rows_at(i, size):
    return pl.ds(pl.multiple_of(i * size, size), size)


def layer_kernel(names, *refs):
    r = SimpleNamespace(**dict(zip(names, refs)))
    rows, width = r.tok.shape
    half = rows // 2
    sub = half // CHUNKS
    heads = r.probs.shape[0]
    units = r.w_up_v.shape[1]
    n_u = units // W
    n_q = r.w_qkv_v.shape[1] // W
    scaling = 1.0 / math.sqrt(HD)
    place, seat = lax.axis_index("dp"), lax.axis_index("tensor")
    z, x = place // 2, place % 2
    y, core = seat // 2, seat % 2
    other_x = {"dp": z * 2 + 1 - x}
    above, below = {"dp": place + 2}, {"dp": place - 2}
    other_core = {"tensor": y * 2 + 1 - core}
    other_y = {"tensor": (1 - y) * 2 + core}

    loads = {}
    pairs = [
        ("tok", "tokens"),
        ("w_qkv_v", "w_qkv"),
        ("cot", "cotangent"),
        ("w_dense_v", "w_dense"),
        ("w_down_v", "w_down"),
        ("w_up_v", "w_up"),
    ]
    for i, (dst, src) in enumerate(pairs):
        loads[dst] = pltpu.make_async_copy(getattr(r, src), getattr(r, dst), r.load_sem.at[i])
        loads[dst].start()

    barrier = pltpu.get_barrier_semaphore()
    for step in range(1, 8):
        peer = {"dp": (place + step) % 8}
        pl.semaphore_signal(barrier, inc=1, device_id=peer, device_id_type=MESH)
    pl.semaphore_signal(barrier, inc=1, device_id=other_core, device_id_type=MESH)
    pl.semaphore_signal(barrier, inc=1, device_id=other_y, device_id_type=MESH)

    def send(src, dst, send_sem, recv_sem, device):
        return pltpu.make_async_remote_copy(
            src_ref=src,
            dst_ref=dst,
            send_sem=send_sem,
            recv_sem=recv_sem,
            device_id=device,
            device_id_type=MESH,
        )

    def act_send(k):
        return send(r.act_s.at[k], r.act_r.at[k], r.act_ss.at[k], r.act_rs.at[k], other_x)

    def gu_send(k):
        return send(r.gu_s.at[k], r.gu_r.at[k], r.gu_ss.at[k], r.gu_rs.at[k], other_x)

    def gj_send(k):
        return send(r.gj_s.at[k], r.gj_r.at[k], r.gj_ss.at[k], r.gj_rs.at[k], other_x)

    def ctx_send():
        return send(r.ctx_s, r.ctx_r, r.ctx_ss, r.ctx_rs, other_x)

    def blk_send(n, i):
        return send(
            r.blk_s.at[n % 2, i], r.blk_r.at[n, 2 * core + i], r.bs.at[n, i], r.br.at[n, i], other_x
        )

    def blk_pass(n, i):
        part = r.blk_r.at[n, 2 * core + i]
        return send(part, part, r.fs.at[n, i], r.fr.at[n, i], other_core)

    def column(t, side):
        return pl.ds(pl.multiple_of((2 * t + side) * B, B), B)

    def fill_blocks(n, source):
        for i in range(2):
            r.blk_s[n % 2, i] = source[:, column(2 * core + i, 1 - x)].astype(f32)

    def start_blocks(n):
        for i in range(2):
            blk_send(n, i).start()

    def pass_blocks(n):
        for i in range(2):
            blk_send(n, i).wait_recv()
            blk_pass(n, i).start()

    def take_blocks(n):
        for i in range(2):
            blk_pass(n, i).wait_recv()

    def partial(a):
        return r.part_m if a == MIX else r.part_a

    def total(a):
        return r.sum_m if a == MIX else r.sum_a

    def own(k):
        return pl.ds(pl.multiple_of(core * half + k * sub, sub), sub)

    def its(k):
        return pl.ds(pl.multiple_of((1 - core) * half + k * sub, sub), sub)

    def near_copy(a, k):
        return send(
            partial(a).at[its(k), :], r.near.at[a, k], r.cs.at[a, k], r.cr.at[a, k], other_core
        )

    def far_copy(a, k):
        return send(r.near.at[a, k], r.far.at[a, k], r.ys.at[a, k], r.yr.at[a, k], other_y)

    def back_copy(a, k):
        part = total(a).at[own(k), :]
        return send(part, part, r.ks.at[a, k], r.kr.at[a, k], other_core)

    def make_partial(a, terms):
        dst = partial(a)
        for side in (1, 0):
            start = pl.multiple_of((core if side == 0 else 1 - core) * half, half)
            at = pl.ds(start, half)
            loop(width // W, lambda n: dst.__setitem__((at, rows_at(n, W)), terms(at, n)))
            if side:
                for k in range(CHUNKS):
                    near_copy(a, k).start()

    def open_sum(a):
        for k in range(CHUNKS):
            near_copy(a, k).wait_recv()
            r.near[a, k] = r.near[a, k] + partial(a)[own(k), :]
            far_copy(a, k).start()

    def close_sum(a, k):
        far_copy(a, k).wait_recv()
        total(a)[own(k), :] = r.near[a, k] + r.far[a, k]
        back_copy(a, k).start()

    def close_all(a, work):
        for k in range(CHUNKS):
            close_sum(a, k)
            work(core * half + k * sub)
            if k:
                back_copy(a, k - 1).wait_recv()
                work((1 - core) * half + (k - 1) * sub)
        back_copy(a, CHUNKS - 1).wait_recv()
        work((1 - core) * half + (CHUNKS - 1) * sub)

    def gather(v, values, at=None):
        part = values[0:8]
        for i in range(1, values.shape[0] // 8):
            part = part + values[8 * i : 8 * i + 8]
        if at is None:
            r.acc[v] = r.acc[v] + part
        else:
            r.acc[v, :, at] = r.acc[v, :, at] + part

    chunks = (
        [("down", k) for k in range(n_u)]
        + [("up", k) for k in range(n_u)]
        + [("dense", 0)]
        + [("qkv", k) for k in range(n_q)]
    )
    slots, tall, wide = [], 0, 0
    for kind, k in chunks:
        if kind in ("down", "dense"):
            slots.append((r.own_t, r.in_t, r.end_t, tall))
            tall += 1
        else:
            slots.append((r.own_w, r.in_w, r.end_w, wide))
            wide += 1

    def up(j, t):
        mine, into, _, n = slots[j]
        return send(mine.at[n, t], into.at[n, t], r.us.at[j, t], r.ur.at[j, t], above)

    def down(j, t, last):
        mine, into, end, n = slots[j]
        dst = end.at[n] if last else into.at[n, t]
        return send(mine.at[n, t], dst, r.ds.at[j, t], r.dr.at[j, t], below)

    def product(j):
        kind, k = chunks[j]
        mine, _, _, n = slots[j]
        if kind == "down":
            act_send(k).wait_recv()
            value = contract(r.act_b[k], r.right[:rows], 0, 0) + contract(
                r.act_r[k].astype(bf16), r.right[rows:], 0, 0
            )
        elif kind == "dense":
            value = contract(r.ctx_b[...], r.right[:rows], 0, 0) + contract(
                r.ctx_r[...].astype(bf16), r.right[rows:], 0, 0
            )
        else:
            if kind == "up":
                gu_send(k).wait_recv()
                left, here, there = r.left_u, r.gu_b[k], r.gu_r[k].astype(bf16)
            else:
                gj_send(k).wait_recv()
                left, here, there = r.left_q, r.gj_b[k], r.gj_r[k].astype(bf16)
            value = contract(left[:, :rows], here, 1, 0) + contract(left[:, rows:], there, 1, 0)
        for t in range(4):
            if kind in ("down", "dense"):
                mine[n, t] = value[:, t * B : (t + 1) * B]
            else:
                mine[n, t] = value[t * B : (t + 1) * B]

        @pl.when(z == 0)
        def _():
            for t in (3, 2, 1):
                up(j, t).start()

        @pl.when(z == 3)
        def _():
            for t in (0, 1, 2):
                down(j, t, t == 2).start()

    def relay(j):
        mine, into, _, n = slots[j]
        for t in (3, 2):

            @pl.when((z > 0) & (z < t))
            def _():
                up(j, t).wait_recv()
                mine[n, t] = mine[n, t] + into[n, t]
                up(j, t).start()

        for t in (0, 1):
            for here in (1, 2):
                if here > t:

                    @pl.when(z == here)
                    def _():
                        down(j, t, False).wait_recv()
                        mine[n, t] = mine[n, t] + into[n, t]
                        down(j, t, t == here - 1).start()

    def result_copy(j):
        kind, k = chunks[j]
        mine, _, _, n = slots[j]
        out = getattr(r, "grad_w_" + kind)
        if kind in ("down", "dense"):
            dst = out.at[pl.ds(k * W, W), :]
        else:
            dst = out.at[:, pl.ds(k * W, W)]
        return pltpu.make_async_copy(mine.at[n, z], dst, r.out_sem.at[j])

    def finish(j):
        mine, into, end, n = slots[j]

        @pl.when(z > 0)
        def _():
            up(j, z).wait_recv()
            mine[n, z] = mine[n, z] + into[n, z]

        @pl.when(z < 3)
        def _():
            down(j, z, True).wait_recv()
            mine[n, z] = mine[n, z] + end[n]

        result_copy(j).start()

    r.acc[...] = jnp.zeros_like(r.acc)
    loads["tok"].wait()

    def first_norm(i):
        at = rows_at(i, 32)
        values = r.tok[at, :].astype(f32)
        average = jnp.mean(values, axis=-1, keepdims=True)
        centered = values - average
        inverse = lax.rsqrt(jnp.mean(centered * centered, axis=-1, keepdims=True) + EPSILON)
        r.average1[at, :] = average
        r.inverse1[at, :] = inverse
        r.first_in[at, :] = (centered * inverse * r.gain1[...] + r.shift1[...]).astype(bf16)

    loop(rows // 32, first_norm)
    loads["w_qkv_v"].wait()

    def joined_step(n):
        at = rows_at(n, W)
        value = contract(r.first_in[...], r.w_qkv_v[:, at], 1, 0) + r.bias_qkv[:, at]
        r.joined[:, at] = value.astype(bf16)

    loop(n_q, joined_step)
    pl.semaphore_wait(barrier, 9)
    loads["cot"].wait()
    fill_blocks(COT, r.cot)
    start_blocks(COT)
    fill_blocks(FI, r.first_in)
    start_blocks(FI)

    block = rows // 3
    for h in range(heads):
        start = 3 * h * HD

        def attend(i, h=h, start=start):
            at = rows_at(i, block)
            raw = contract(
                r.joined[at, start : start + HD], r.joined[:, start + HD : start + 2 * HD], 1, 1
            )
            here = lax.broadcasted_iota(jnp.int32, (block, rows), 0) + i * block
            there = lax.broadcasted_iota(jnp.int32, (block, rows), 1)
            allowed = (r.seg_col[at, :] == r.seg_row[...]) & (there <= here)
            bias = r.slopes[h] * (there - here).astype(f32)
            scores = jnp.where(allowed, raw * scaling + bias, -1e30)
            weights = jnp.exp(scores - jnp.max(scores, axis=-1, keepdims=True))
            prob = weights / jnp.sum(weights, axis=-1, keepdims=True)
            r.probs[h, at, :] = prob
            value = contract(
                prob.astype(bf16), r.joined[:, start + 2 * HD : start + 3 * HD], 1, 0
            ).astype(bf16)
            r.ctx_b[at, h * HD : (h + 1) * HD] = value

        loop(3, attend)
    r.ctx_s[...] = r.ctx_b[...].astype(f32)
    ctx_send().start()
    loads["w_dense_v"].wait()
    make_partial(ATT, lambda at, n: contract(r.ctx_b[at, :], r.w_dense_v[:, rows_at(n, W)], 1, 0))
    open_sum(ATT)

    loads["w_down_v"].wait()

    def early(k):
        at = rows_at(k, W)
        r.broad[:, at] = contract(r.cot[...], r.w_down_v[at, :], 1, 1)

    loop(n_u, early)
    loop(rows // 16, lambda i: gather(BDOWN, r.cot[rows_at(i, 16), :].astype(f32)))
    pass_blocks(COT)
    for t in range(4):
        r.right[:rows, t * B : (t + 1) * B] = r.cot[:, column(t, x)]
        r.left_q[t * B : (t + 1) * B, :rows] = (
            r.first_in[:, column(t, x)].astype(f32).T.astype(bf16)
        )
    pass_blocks(FI)
    take_blocks(COT)
    take_blocks(FI)
    for t in range(4):
        r.right[rows:, t * B : (t + 1) * B] = r.blk_r[COT, t].astype(bf16)
        r.left_q[t * B : (t + 1) * B, rows:] = r.blk_r[FI, t].T.astype(bf16)

    def second_norm(start):
        def body(i):
            at = pl.ds(pl.multiple_of(start + i * 16, 16), 16)
            values = r.tok[at, :].astype(f32) + r.sum_a[at, :] + r.bias_dense[...]
            average = jnp.mean(values, axis=-1, keepdims=True)
            centered = values - average
            inverse = lax.rsqrt(jnp.mean(centered * centered, axis=-1, keepdims=True) + EPSILON)
            r.hidden[at, :] = values
            r.average2[at, :] = average
            r.inverse2[at, :] = inverse
            r.second_in[at, :] = (centered * inverse * r.gain2[...] + r.shift2[...]).astype(bf16)

        loop(sub // 16, body)

    close_all(ATT, second_norm)

    loads["w_up_v"].wait()
    for k in range(n_u):
        columns = slice(k * W, (k + 1) * W)
        r.act_s[k] = contract(r.second_in[...], r.w_up_v[:, columns], 1, 0) + r.bias_up[:, columns]

        def gelu_step(i, k=k, columns=columns):
            at = rows_at(i, 32)
            value, slope = gelu_pair(r.act_s[k, at, :])
            r.act_s[k, at, :] = value
            r.act_b[k, at, :] = value.astype(bf16)
            change = r.broad[at, columns] * slope
            r.gu_s[k, at, :] = change
            r.gu_b[k, at, :] = change.astype(bf16)
            gather(BUP, change, columns)

        loop(rows // 32, gelu_step)
        act_send(k).start()
    for i in range(2):
        blk_send(COT, i).wait_send()
    fill_blocks(SI, r.second_in)
    start_blocks(SI)
    for k in range(n_u):
        gu_send(k).start()

    def up_terms(at, n):
        return sum(
            contract(r.gu_b[k, at, :], r.w_up_v[rows_at(n, W), k * W : (k + 1) * W], 1, 1)
            for k in range(n_u)
        )

    def mixed_terms(at, n):
        return sum(
            contract(r.act_b[k, at, :], r.w_down_v[k * W : (k + 1) * W, rows_at(n, W)], 1, 0)
            for k in range(n_u)
        )

    for k in range(CHUNKS):
        near_copy(ATT, k).wait_send()
    make_partial(GN2, up_terms)
    for k in range(CHUNKS):
        back_copy(ATT, k).wait_send()
    open_sum(GN2)
    make_partial(MIX, mixed_terms)
    open_sum(MIX)
    for t in range(4):
        r.left_u[t * B : (t + 1) * B, :rows] = (
            r.second_in[:, column(t, x)].astype(f32).T.astype(bf16)
        )
    product(0)
    product(1)
    relay(0)

    def hidden_step(start):
        def body(i):
            at = pl.ds(pl.multiple_of(start + i * 16, 16), 16)
            upstream = r.sum_a[at, :]
            normed = (r.hidden[at, :] - r.average2[at, :]) * r.inverse2[at, :]
            change = norm_backward(upstream, normed, r.inverse2[at, :], r.gain2[...])
            value = r.cot[at, :].astype(f32) + change
            r.broad[at, :] = value
            r.gh_b[at, :] = value.astype(bf16)
            gather(GAIN2, upstream * normed)
            gather(SHIFT2, upstream)
            gather(BDENSE, value)

        loop(sub // 16, body)

    close_all(GN2, hidden_step)
    for i in range(2):
        blk_send(FI, i).wait_send()
    fill_blocks(GH, r.gh_b)
    start_blocks(GH)
    r.gctx[...] = contract(r.gh_b[...], r.w_dense_v[...], 1, 1).astype(bf16)
    product(2)
    relay(1)

    for h in range(heads):
        start = 3 * h * HD
        queries = r.joined[:, start : start + HD]
        key_vecs = r.joined[:, start + HD : start + 2 * HD]
        val_vecs = r.joined[:, start + 2 * HD : start + 3 * HD]
        upstream = r.gctx[:, h * HD : (h + 1) * HD]
        prob = r.probs[h]
        grad_probs = contract(upstream, val_vecs, 1, 1)
        row_inner = jnp.sum(prob * grad_probs, axis=-1, keepdims=True)
        grad_scores = (prob * (grad_probs - row_inner)).astype(bf16)
        thirds = (
            contract(grad_scores, key_vecs, 1, 0) * scaling,
            contract(grad_scores, queries, 0, 0) * scaling,
            contract(prob.astype(bf16), upstream, 0, 0),
        )
        for third, value in enumerate(thirds):
            k, offset = divmod(start + third * HD, W)
            r.gj_s[k, :, offset : offset + HD] = value
    for k in range(n_q):
        gj_send(k).start()

        def joined_grad(i, k=k):
            at = rows_at(i, 32)
            value = r.gj_s[k, at, :]
            r.gj_b[k, at, :] = value.astype(bf16)
            gather(BQKV, value, slice(k * W, (k + 1) * W))

        loop(rows // 32, joined_grad)

    def joined_terms(at, n):
        return sum(
            contract(r.gj_b[k, at, :], r.w_qkv_v[rows_at(n, W), k * W : (k + 1) * W], 1, 1)
            for k in range(n_q)
        )

    for k in range(CHUNKS):
        near_copy(GN2, k).wait_send()
        back_copy(GN2, k).wait_send()
    make_partial(GN1, joined_terms)
    open_sum(GN1)
    product(3)
    relay(2)

    pass_blocks(SI)
    take_blocks(SI)
    for t in range(4):
        r.left_u[t * B : (t + 1) * B, rows:] = r.blk_r[SI, t].T.astype(bf16)

    def output_step(start):
        def body(i):
            at = pl.ds(pl.multiple_of(start + i * 16, 16), 16)
            value = r.hidden[at, :] + r.sum_m[at, :] + r.bias_down[...]
            r.second_in[at, :] = value.astype(bf16)

        loop(sub // 16, body)

    close_all(MIX, output_step)
    output_copy = pltpu.make_async_copy(r.second_in, r.output, r.load_sem.at[0])
    output_copy.start()
    product(4)
    relay(3)
    product(5)
    relay(4)
    finish(0)

    def input_step(start):
        def body(i):
            at = pl.ds(pl.multiple_of(start + i * 16, 16), 16)
            upstream = r.sum_a[at, :]
            inverse = r.inverse1[at, :]
            normed = (r.tok[at, :].astype(f32) - r.average1[at, :]) * inverse
            change = norm_backward(upstream, normed, inverse, r.gain1[...])
            gather(GAIN1, upstream * normed)
            gather(SHIFT1, upstream)
            r.broad[at, :] = r.broad[at, :] + change

        loop(sub // 16, body)

    close_all(GN1, input_step)
    input_copy = pltpu.make_async_copy(r.broad, r.grad_input, r.load_sem.at[1])
    input_copy.start()

    for v in range(8):
        vector = jnp.sum(r.acc[v], axis=0, keepdims=True)
        if v == BQKV:
            piece = n_q * W // 8
        else:
            piece = B
        for p in range(8):
            r.table[p, v : v + 1, :piece] = vector[:, p * piece : (p + 1) * piece]

    def vector_send(step):
        peer = (place + step) % 8
        return send(
            r.table.at[peer], r.vec_r.at[step], r.vs.at[step], r.vr.at[step], {"dp": peer}
        )

    for step in range(1, 8):
        vector_send(step).start()
    product(6)
    relay(5)
    finish(1)
    product(7)
    relay(6)
    finish(2)
    finish(3)
    pass_blocks(GH)
    for t in range(4):
        r.right[:rows, t * B : (t + 1) * B] = r.gh_b[:, column(t, x)]
    take_blocks(GH)
    for t in range(4):
        r.right[rows:, t * B : (t + 1) * B] = r.blk_r[GH, t].astype(bf16)
    ctx_send().wait_recv()
    product(8)
    relay(7)
    finish(4)
    vector = r.table[place]
    for step in range(1, 8):
        vector_send(step).wait_recv()
        vector = vector + r.vec_r[step]
    r.vectors[...] = vector
    product(9)
    relay(8)
    finish(5)
    product(10)
    relay(9)
    finish(6)
    product(11)
    relay(10)
    relay(11)
    for j in range(7, 12):
        finish(j)

    for k in range(n_u):
        act_send(k).wait_send()
        gu_send(k).wait_send()
    for k in range(n_q):
        gj_send(k).wait_send()
    ctx_send().wait_send()
    for n in range(4):
        for i in range(2):
            if n in (SI, GH):
                blk_send(n, i).wait_send()
            blk_pass(n, i).wait_send()
    for a in range(SUMS):
        for k in range(CHUNKS):
            if a in (MIX, GN1):
                near_copy(a, k).wait_send()
                back_copy(a, k).wait_send()
            far_copy(a, k).wait_send()
    for step in range(1, 8):
        vector_send(step).wait_send()
    for j in range(len(chunks)):
        for t in range(4):

            @pl.when(z < t)
            def _():
                up(j, t).wait_send()

            @pl.when(z > t)
            def _():
                down(j, t, False).wait_send()

        result_copy(j).wait()
    output_copy.wait()
    input_copy.wait()


def whole_layer(tokens, segment_ids, cotangent, *rest):
    (
        norm1_gain,
        norm1_shift,
        w_qkv,
        b_qkv,
        w_dense,
        b_dense,
        norm2_gain,
        norm2_shift,
        w_up,
        b_up,
        w_down,
        b_down,
    ) = rest
    rows, width = tokens.shape
    joined = w_qkv.shape[1]
    heads = joined // (3 * HD)
    inner = heads * HD
    units = w_up.shape[1]
    n_u, n_q = units // W, joined // W
    n_wide = n_u + n_q
    n_all = N_TALL + n_wide
    sub = rows // 2 // CHUNKS
    head_start = lax.axis_index("tensor") * heads
    slopes = 2.0 ** (-8.0 * (head_start + jnp.arange(heads) + 1).astype(f32) / H)
    slopes = jnp.broadcast_to(slopes[:, None, None], (heads, 1, rows))
    inputs = [
        ("seg_row", segment_ids),
        ("seg_col", segment_ids.reshape(rows, 1)),
        ("slopes", slopes),
        ("gain1", norm1_gain[None]),
        ("shift1", norm1_shift[None]),
        ("bias_qkv", b_qkv[None]),
        ("bias_dense", b_dense[None]),
        ("gain2", norm2_gain[None]),
        ("shift2", norm2_shift[None]),
        ("bias_up", b_up[None]),
        ("bias_down", b_down[None]),
        ("tokens", tokens),
        ("cotangent", cotangent),
        ("w_qkv", w_qkv),
        ("w_dense", w_dense),
        ("w_up", w_up),
        ("w_down", w_down),
    ]
    small = 11
    outs = [
        ("output", (rows, width), bf16),
        ("grad_input", (rows, width), f32),
        ("grad_w_qkv", (width // 8, joined), f32),
        ("grad_w_dense", (inner, width // 8), f32),
        ("grad_w_up", (width // 8, units), f32),
        ("grad_w_down", (units, width // 8), f32),
        ("vectors", (8, B), f32),
    ]
    dma = pltpu.SemaphoreType.DMA
    scratch = [
        ("tok", (rows, width), bf16),
        ("cot", (rows, width), bf16),
        ("w_qkv_v", w_qkv.shape, bf16),
        ("w_dense_v", w_dense.shape, bf16),
        ("w_up_v", w_up.shape, bf16),
        ("w_down_v", w_down.shape, bf16),
        ("average1", (rows, 1), f32),
        ("inverse1", (rows, 1), f32),
        ("average2", (rows, 1), f32),
        ("inverse2", (rows, 1), f32),
        ("first_in", (rows, width), bf16),
        ("second_in", (rows, width), bf16),
        ("hidden", (rows, width), f32),
        ("broad", (rows, width), f32),
        ("gh_b", (rows, width), bf16),
        ("joined", (rows, joined), bf16),
        ("probs", (heads, rows, rows), f32),
        ("ctx_b", (rows, inner), bf16),
        ("gctx", (rows, inner), bf16),
        ("act_b", (n_u, rows, W), bf16),
        ("gu_b", (n_u, rows, W), bf16),
        ("gj_b", (n_q, rows, W), bf16),
        ("act_s", (n_u, rows, W), f32),
        ("act_r", (n_u, rows, W), f32),
        ("gu_s", (n_u, rows, W), f32),
        ("gu_r", (n_u, rows, W), f32),
        ("gj_s", (n_q, rows, W), f32),
        ("gj_r", (n_q, rows, W), f32),
        ("ctx_s", (rows, inner), f32),
        ("ctx_r", (rows, inner), f32),
        ("blk_s", (2, 2, rows, B), f32),
        ("blk_r", (4, 4, rows, B), f32),
        ("right", (2 * rows, 4 * B), bf16),
        ("left_u", (4 * B, 2 * rows), bf16),
        ("left_q", (4 * B, 2 * rows), bf16),
        ("part_a", (rows, width), f32),
        ("part_m", (rows, width), f32),
        ("sum_a", (rows, width), f32),
        ("sum_m", (rows, width), f32),
        ("near", (SUMS, CHUNKS, sub, width), f32),
        ("far", (SUMS, CHUNKS, sub, width), f32),
        ("own_t", (N_TALL, 4, W, B), f32),
        ("in_t", (N_TALL, 4, W, B), f32),
        ("end_t", (N_TALL, W, B), f32),
        ("own_w", (n_wide, 4, B, W), f32),
        ("in_w", (n_wide, 4, B, W), f32),
        ("end_w", (n_wide, B, W), f32),
        ("acc", (8, 8, width), f32),
        ("table", (8, 8, B), f32),
        ("vec_r", (8, 8, B), f32),
    ]
    sems = [
        ("load_sem", (6,)),
        ("out_sem", (n_all,)),
        ("act_ss", (n_u,)),
        ("act_rs", (n_u,)),
        ("gu_ss", (n_u,)),
        ("gu_rs", (n_u,)),
        ("gj_ss", (n_q,)),
        ("gj_rs", (n_q,)),
        ("ctx_ss", None),
        ("ctx_rs", None),
        ("bs", (4, 2)),
        ("br", (4, 2)),
        ("fs", (4, 2)),
        ("fr", (4, 2)),
        ("cs", (SUMS, CHUNKS)),
        ("cr", (SUMS, CHUNKS)),
        ("ys", (SUMS, CHUNKS)),
        ("yr", (SUMS, CHUNKS)),
        ("ks", (SUMS, CHUNKS)),
        ("kr", (SUMS, CHUNKS)),
        ("us", (n_all, 4)),
        ("ur", (n_all, 4)),
        ("ds", (n_all, 4)),
        ("dr", (n_all, 4)),
        ("vs", (8,)),
        ("vr", (8,)),
    ]
    names = [n for n, _ in inputs] + [o[0] for o in outs] + [s[0] for s in scratch]
    names += [n for n, _ in sems]
    vmem, anywhere = pl.BlockSpec(memory_space=pltpu.VMEM), pl.BlockSpec(memory_space=pl.ANY)
    results = pl.pallas_call(
        functools.partial(layer_kernel, names),
        out_shape=[jax.ShapeDtypeStruct(shape, kind) for _, shape, kind in outs],
        in_specs=[vmem] * small + [anywhere] * (len(inputs) - small),
        out_specs=[anywhere] * (len(outs) - 1) + [vmem],
        scratch_shapes=[pltpu.VMEM(shape, kind) for _, shape, kind in scratch]
        + [dma(shape) if shape else dma for _, shape in sems],
        compiler_params=pltpu.CompilerParams(
            collective_id=7, has_side_effects=True, vmem_limit_bytes=63 * MIB
        ),
    )(*[value for _, value in inputs])
    output, grad_input, g_qkv, g_dense, g_up, g_down, vectors = results
    v = [vectors[i] for i in range(8)]
    return (
        output,
        grad_input,
        v[GAIN1],
        v[SHIFT1],
        g_qkv,
        v[BQKV][: joined // 8],
        g_dense,
        v[BDENSE],
        v[GAIN2],
        v[SHIFT2],
        g_up,
        v[BUP],
        g_down,
        v[BDOWN],
    )


def solution(mesh):
    in_specs = (
        P("dp", None),
        P("dp", None),
        P("dp", None),
        P(),
        P(),
        P(None, "tensor"),
        P("tensor"),
        P("tensor", None),
        P(),
        P(),
        P(),
        P(None, "tensor"),
        P("tensor"),
        P("tensor", None),
        P(),
    )
    out_specs = (
        P("dp", None),
        P("dp", None),
        P("dp"),
        P("dp"),
        P("dp", "tensor"),
        P(("tensor", "dp")),
        P("tensor", "dp"),
        P("dp"),
        P("dp"),
        P("dp"),
        P("dp", "tensor"),
        P(("tensor", "dp")),
        P("tensor", "dp"),
        P("dp"),
    )
    sizes = (mesh.shape["dp"], mesh.shape["tensor"])
    body = whole_layer if sizes == (8, 4) else functools.partial(local, sizes)
    return jax.shard_map(body, mesh=mesh, in_specs=in_specs, out_specs=out_specs, check_vma=False)
```

```python
import functools
import math
from types import SimpleNamespace

import jax
import jax.numpy as jnp
from jax import lax
from jax.experimental import pallas as pl
from jax.experimental.pallas import tpu as pltpu
from jax.sharding import PartitionSpec as P

H = 16
HD = 64


EPSILON = 1e-05
GELU_COEF = math.sqrt(2.0 / math.pi)


def layer_norm(values, gain, shift):
    average = jnp.mean(values, axis=-1, keepdims=True)
    centered = values - average
    variance = jnp.mean(centered * centered, axis=-1, keepdims=True)
    inverse = lax.rsqrt(variance + EPSILON)
    normed = centered * inverse
    return (normed * gain + shift, normed, inverse)


def norm_backward(upstream, normed, inverse, gain):
    scaled = upstream * gain
    return inverse * (
        scaled
        - jnp.mean(scaled, axis=-1, keepdims=True)
        - normed * jnp.mean(scaled * normed, axis=-1, keepdims=True)
    )


def gelu_pair(inputs):
    tangent = jnp.tanh(GELU_COEF * (inputs + 0.044715 * inputs * inputs * inputs))
    result = 0.5 * inputs * (1.0 + tangent)
    derivative = 0.5 * (1.0 + tangent) + 0.5 * inputs * (1.0 - tangent * tangent) * GELU_COEF * (
        1.0 + 3.0 * 0.044715 * inputs * inputs
    )
    return (result, derivative)


def head_scores(queries, key_vecs, slopes, offset, allowed, scaling):
    raw_scores = jnp.einsum("ihe,jhe->hij", queries, key_vecs, preferred_element_type=jnp.float32)
    return jnp.where(
        allowed[None], raw_scores * scaling + slopes[:, None, None] * offset[None], -1e30
    )

CHUNKS = 4
MESH = pl.DeviceIdType.MESH
MIB = 1024 * 1024


def scatter(grads, kinds):
    return [
        lax.psum_scatter(g, "dp", scatter_dimension=0 if k == "rows" else 1, tiled=True)
        for g, k in zip(grads, kinds)
    ]


def scatter_vectors(vectors, n_dp):
    widths = [v.shape[0] // n_dp for v in vectors]
    widest = -(-max(widths) // 128) * 128
    table = jnp.stack(
        [jnp.pad(v.reshape(n_dp, -1), ((0, 0), (0, widest - w))) for v, w in zip(vectors, widths)],
        axis=1,
    ).reshape(n_dp * len(vectors), widest)
    (mine,) = scatter([table], ["rows"])
    return [mine[i, :w] for i, w in enumerate(widths)]


def local(
    sizes,
    tokens,
    segment_ids,
    cotangent,
    norm1_gain,
    norm1_shift,
    w_qkv,
    b_qkv,
    w_dense,
    b_dense,
    norm2_gain,
    norm2_shift,
    w_up,
    b_up,
    w_down,
    b_down,
):
    segments = segment_ids[0]
    row_count = tokens.shape[0]
    heads_here = w_qkv.shape[1] // (3 * HD)
    head_start = lax.axis_index("tensor") * heads_here
    scaling = 1.0 / math.sqrt(HD)
    slopes = 2.0 ** (-8.0 * (head_start + jnp.arange(heads_here) + 1).astype(jnp.float32) / H)
    places = jnp.arange(row_count)
    offset = (places[None, :] - places[:, None]).astype(jnp.float32)
    allowed = (segments[:, None] == segments[None, :]) & (places[None, :] <= places[:, None])
    inputs = tokens.astype(jnp.float32)
    first_out, normed1, inverse1 = layer_norm(inputs, norm1_gain, norm1_shift)
    first_in = first_out.astype(jnp.bfloat16)
    joined = (jnp.dot(first_in, w_qkv, preferred_element_type=jnp.float32) + b_qkv).astype(
        jnp.bfloat16
    )
    joined = joined.reshape(row_count, heads_here, 3, HD)
    queries = joined[:, :, 0]
    key_vecs = joined[:, :, 1]
    val_vecs = joined[:, :, 2]
    scores = head_scores(queries, key_vecs, slopes, offset, allowed, scaling)
    highest = jnp.max(scores, axis=-1, keepdims=True)
    log_total = highest + jnp.log(jnp.sum(jnp.exp(scores - highest), axis=-1, keepdims=True))
    probs = jnp.exp(scores - log_total)
    probs_b = probs.astype(jnp.bfloat16)
    context = jnp.einsum(
        "hij,jhe->ihe", probs_b, val_vecs, preferred_element_type=jnp.float32
    ).astype(jnp.bfloat16)
    context = context.reshape(row_count, heads_here * HD)
    attended = lax.psum(jnp.dot(context, w_dense, preferred_element_type=jnp.float32), "tensor")
    hidden = inputs + attended + b_dense
    second_out, normed2, inverse2 = layer_norm(hidden, norm2_gain, norm2_shift)
    second_in = second_out.astype(jnp.bfloat16)
    upward = jnp.dot(second_in, w_up, preferred_element_type=jnp.float32) + b_up
    activated, gelu_slope = gelu_pair(upward)
    activated_b = activated.astype(jnp.bfloat16)
    mixed = jnp.dot(activated_b, w_down, preferred_element_type=jnp.float32)
    grad_out = cotangent.astype(jnp.float32)
    grad_w_down = jnp.dot(activated_b.T, cotangent, preferred_element_type=jnp.float32)
    grad_b_down = jnp.sum(grad_out, axis=0)
    grad_up = jnp.dot(cotangent, w_down.T, preferred_element_type=jnp.float32) * gelu_slope
    grad_up_b = grad_up.astype(jnp.bfloat16)
    grad_w_up = jnp.dot(second_in.T, grad_up_b, preferred_element_type=jnp.float32)
    grad_b_up = jnp.sum(grad_up, axis=0)
    grad_norm2 = jnp.dot(grad_up_b, w_up.T, preferred_element_type=jnp.float32)
    grad_norm2 = lax.psum(grad_norm2, "tensor")
    mixed = lax.psum(mixed, "tensor")
    grad_hidden = grad_out + norm_backward(grad_norm2, normed2, inverse2, norm2_gain)
    grad_hidden_b = grad_hidden.astype(jnp.bfloat16)
    grad_w_dense = jnp.dot(context.T, grad_hidden_b, preferred_element_type=jnp.float32)
    grad_context = jnp.dot(grad_hidden_b, w_dense.T, preferred_element_type=jnp.float32).astype(
        jnp.bfloat16
    )
    grad_context = grad_context.reshape(row_count, heads_here, HD)
    scores_again = head_scores(queries, key_vecs, slopes, offset, allowed, scaling)
    probs_again = jnp.exp(scores_again - log_total)
    probs_again_b = probs_again.astype(jnp.bfloat16)
    grad_vals = jnp.einsum(
        "hij,ihe->jhe", probs_again_b, grad_context, preferred_element_type=jnp.float32
    )
    grad_probs = jnp.einsum(
        "ihe,jhe->hij", grad_context, val_vecs, preferred_element_type=jnp.float32
    )
    row_inner = jnp.sum(probs_again * grad_probs, axis=-1, keepdims=True)
    grad_scores = (probs_again * (grad_probs - row_inner)).astype(jnp.bfloat16)
    grad_queries = (
        jnp.einsum("hij,jhe->ihe", grad_scores, key_vecs, preferred_element_type=jnp.float32)
        * scaling
    )
    grad_keys = (
        jnp.einsum("hij,ihe->jhe", grad_scores, queries, preferred_element_type=jnp.float32)
        * scaling
    )
    grad_joined = jnp.stack([grad_queries, grad_keys, grad_vals], axis=2).reshape(
        row_count, 3 * heads_here * HD
    )
    grad_joined_b = grad_joined.astype(jnp.bfloat16)
    grad_w_qkv = jnp.dot(first_in.T, grad_joined_b, preferred_element_type=jnp.float32)
    grad_norm1 = jnp.dot(grad_joined_b, w_qkv.T, preferred_element_type=jnp.float32)
    grad_norm1 = lax.psum(grad_norm1, "tensor")
    grad_w_up, grad_w_down, grad_w_qkv, grad_w_dense = scatter(
        [grad_w_up, grad_w_down, grad_w_qkv, grad_w_dense],
        ["rows", "columns", "rows", "columns"],
    )
    output = (hidden + mixed + b_down).astype(jnp.bfloat16)
    grad_gain2 = jnp.sum(grad_norm2 * normed2, axis=0)
    grad_shift2 = jnp.sum(grad_norm2, axis=0)
    grad_b_dense = jnp.sum(grad_hidden, axis=0)
    grad_b_qkv = jnp.sum(grad_joined, axis=0)
    grad_gain1 = jnp.sum(grad_norm1 * normed1, axis=0)
    grad_shift1 = jnp.sum(grad_norm1, axis=0)
    grad_input = grad_hidden + norm_backward(grad_norm1, normed1, inverse1, norm1_gain)
    vectors = scatter_vectors(
        [
            grad_gain1,
            grad_shift1,
            grad_b_qkv,
            grad_b_dense,
            grad_gain2,
            grad_shift2,
            grad_b_up,
            grad_b_down,
        ],
        sizes[0],
    )
    gain1, shift1, b_qkv_part, b_dense_part, gain2, shift2, b_up_part, b_down_part = vectors
    return (
        output,
        grad_input,
        gain1,
        shift1,
        grad_w_qkv,
        b_qkv_part,
        grad_w_dense,
        b_dense_part,
        gain2,
        shift2,
        grad_w_up,
        b_up_part,
        grad_w_down,
        b_down_part,
    )


W = 256
B = 128
SUMS = 4
ATT, GN2, MIX, GN1 = range(SUMS)
COT, FI, SI, GH = range(4)
GAIN1, SHIFT1, BQKV, BDENSE, GAIN2, SHIFT2, BUP, BDOWN = range(8)
N_TALL = 5
RELAY, AGAIN, FINISH = 1, 2, 4
f32 = jnp.float32
bf16 = jnp.bfloat16


def contract(left, right, left_axis, right_axis):
    return lax.dot_general(
        left, right, (((left_axis,), (right_axis,)), ((), ())), preferred_element_type=f32
    )


def loop(count, body):
    def step(i, carry):
        body(i)
        return carry

    lax.fori_loop(0, count, step, 0)


def rows_at(i, size):
    return pl.ds(pl.multiple_of(i * size, size), size)


def layer_kernel(names, *refs):
    r = SimpleNamespace(**dict(zip(names, refs)))
    rows, width = r.tok.shape
    half = rows // 2
    sub = half // CHUNKS
    heads = r.probs.shape[0]
    units = r.w_up_v.shape[1]
    n_u = units // W
    n_q = r.w_qkv_v.shape[1] // W
    scaling = 1.0 / math.sqrt(HD)
    place, seat = lax.axis_index("dp"), lax.axis_index("tensor")
    z, x = place // 2, place % 2
    y, core = seat // 2, seat % 2
    other_x = {"dp": z * 2 + 1 - x}
    above, below = {"dp": place + 2}, {"dp": place - 2}
    other_core = {"tensor": y * 2 + 1 - core}
    other_y = {"tensor": (1 - y) * 2 + core}

    loads = {}
    pairs = [
        ("tok", "tokens"),
        ("w_qkv_v", "w_qkv"),
        ("cot", "cotangent"),
        ("w_dense_v", "w_dense"),
        ("w_down_v", "w_down"),
        ("w_up_v", "w_up"),
    ]
    for i, (dst, src) in enumerate(pairs):
        loads[dst] = pltpu.make_async_copy(getattr(r, src), getattr(r, dst), r.load_sem.at[i])
        loads[dst].start()

    barrier = pltpu.get_barrier_semaphore()
    for step in range(1, 8):
        peer = {"dp": (place + step) % 8}
        pl.semaphore_signal(barrier, inc=1, device_id=peer, device_id_type=MESH)
    pl.semaphore_signal(barrier, inc=1, device_id=other_core, device_id_type=MESH)
    pl.semaphore_signal(barrier, inc=1, device_id=other_y, device_id_type=MESH)

    def send(src, dst, send_sem, recv_sem, device):
        return pltpu.make_async_remote_copy(
            src_ref=src,
            dst_ref=dst,
            send_sem=send_sem,
            recv_sem=recv_sem,
            device_id=device,
            device_id_type=MESH,
        )

    def act_send(k):
        return send(r.act_s.at[k], r.act_r.at[k], r.act_ss.at[k], r.act_rs.at[k], other_x)

    def gu_send(k):
        return send(r.gu_s.at[k], r.gu_r.at[k], r.gu_ss.at[k], r.gu_rs.at[k], other_x)

    def gj_send(k):
        return send(r.gj_s.at[k], r.gj_r.at[k], r.gj_ss.at[k], r.gj_rs.at[k], other_x)

    def ctx_send():
        return send(r.ctx_s, r.ctx_r, r.ctx_ss, r.ctx_rs, other_x)

    def blk_send(n):
        return send(r.blk_s.at[n % 2], r.blk_r.at[n, seat], r.bs.at[n], r.br.at[n], other_x)

    def blk_pass(n, i):
        part = r.blk_r.at[n, (seat if i < 2 else 2 * (1 - y) + core)]
        device = other_y if i == 1 else other_core
        return send(part, part, r.fs.at[n, i], r.fr.at[n, i], device)

    def column(t, side):
        return pl.ds(pl.multiple_of((2 * t + side) * B, B), B)

    def start_block(n, source):
        r.blk_s[n % 2] = source[:, column(seat, 1 - x)].astype(f32)
        blk_send(n).start()

    def pass_block(n):
        blk_send(n).wait_recv()
        blk_pass(n, 0).start()
        blk_pass(n, 1).start()

    def take_block(n):
        blk_pass(n, 1).wait_recv()
        blk_pass(n, 2).start()
        blk_pass(n, 0).wait_recv()
        blk_pass(n, 2).wait_recv()

    def partial(a):
        return r.part_m if a == MIX else r.part_a

    def total(a):
        return r.sum_m if a == MIX else r.sum_a

    def own(k):
        return pl.ds(pl.multiple_of(core * half + k * sub, sub), sub)

    def its(k):
        return pl.ds(pl.multiple_of((1 - core) * half + k * sub, sub), sub)

    def near_copy(a, k):
        return send(
            partial(a).at[its(k), :], r.near.at[a, k], r.cs.at[a, k], r.cr.at[a, k], other_core
        )

    def far_copy(a, k):
        return send(r.near.at[a, k], r.far.at[a, k], r.ys.at[a, k], r.yr.at[a, k], other_y)

    def back_copy(a, k):
        part = total(a).at[own(k), :]
        return send(part, part, r.ks.at[a, k], r.kr.at[a, k], other_core)

    def make_partial(a, terms):
        dst = partial(a)
        for side in (1, 0):
            start = pl.multiple_of((core if side == 0 else 1 - core) * half, half)
            at = pl.ds(start, half)
            loop(width // W, lambda n: dst.__setitem__((at, rows_at(n, W)), terms(at, n)))
            if side:
                for k in range(CHUNKS):
                    near_copy(a, k).start()

    def open_sum(a):
        for k in range(CHUNKS):
            near_copy(a, k).wait_recv()
            r.near[a, k] = r.near[a, k] + partial(a)[own(k), :]
            far_copy(a, k).start()

    def close_sum(a, k):
        far_copy(a, k).wait_recv()
        total(a)[own(k), :] = r.near[a, k] + r.far[a, k]
        back_copy(a, k).start()

    def close_all(a, work):
        for k in range(CHUNKS):
            close_sum(a, k)
            work(core * half + k * sub)
            if k:
                back_copy(a, k - 1).wait_recv()
                work((1 - core) * half + (k - 1) * sub)
        back_copy(a, CHUNKS - 1).wait_recv()
        work((1 - core) * half + (CHUNKS - 1) * sub)

    def gather(v, values, at=None):
        part = values[0:8]
        for i in range(1, values.shape[0] // 8):
            part = part + values[8 * i : 8 * i + 8]
        if at is None:
            r.acc[v] = r.acc[v] + part
        else:
            r.acc[v, :, at] = r.acc[v, :, at] + part

    chunks = (
        [("down", k) for k in range(n_u)]
        + [("up", k) for k in range(n_u)]
        + [("dense", 0)]
        + [("qkv", k) for k in range(n_q)]
    )
    slots, tall, wide = [], 0, 0
    for kind, k in chunks:
        if kind in ("down", "dense"):
            slots.append((r.own_t, r.in_t, r.end_t, tall))
            tall += 1
        else:
            slots.append((r.own_w, r.in_w, r.end_w, wide))
            wide += 1

    def up(j, t):
        mine, into, _, n = slots[j]
        return send(mine.at[n, t], into.at[n, t], r.us.at[j, t], r.ur.at[j, t], above)

    def down(j, t, last):
        mine, into, end, n = slots[j]
        dst = end.at[n] if last else into.at[n, t]
        return send(mine.at[n, t], dst, r.ds.at[j, t], r.dr.at[j, t], below)

    def product(j):
        kind, k = chunks[j]
        mine, _, _, n = slots[j]
        if kind == "down":
            act_send(k).wait_recv()
            value = contract(r.act_b[k], r.right[:rows], 0, 0) + contract(
                r.act_r[k].astype(bf16), r.right[rows:], 0, 0
            )
        elif kind == "dense":
            value = contract(r.ctx_b[...], r.right[:rows], 0, 0) + contract(
                r.ctx_r[...].astype(bf16), r.right[rows:], 0, 0
            )
        else:
            if kind == "up":
                gu_send(k).wait_recv()
                left, here, there = r.left_u, r.gu_b[k], r.gu_r[k].astype(bf16)
            else:
                gj_send(k).wait_recv()
                left, here, there = r.left_q, r.gj_b[k], r.gj_r[k].astype(bf16)
            value = contract(left[:, :rows], here, 1, 0) + contract(left[:, rows:], there, 1, 0)
        for t in range(4):
            if kind in ("down", "dense"):
                mine[n, t] = value[:, t * B : (t + 1) * B]
            else:
                mine[n, t] = value[t * B : (t + 1) * B]

        @pl.when(z == 0)
        def _():
            for t in (3, 2, 1):
                up(j, t).start()

        @pl.when(z == 3)
        def _():
            for t in (0, 1, 2):
                down(j, t, t == 2).start()

    def pass_on(j, t, here, upward):
        mine, into, _, n = slots[j]

        @pl.when(z == here)
        def _():
            came = up(j, t) if upward else down(j, t, False)
            came.wait_recv()
            mine[n, t] = mine[n, t] + into[n, t]
            onward = up(j, t) if upward else down(j, t, t == here - 1)
            onward.start()

    def relay(j):
        pass_on(j, 3, 1, True)
        pass_on(j, 2, 1, True)
        pass_on(j, 0, 2, False)
        pass_on(j, 1, 2, False)

    def relay_again(j):
        pass_on(j, 3, 2, True)
        pass_on(j, 0, 1, False)

    def result_copy(j):
        kind, k = chunks[j]
        mine, _, _, n = slots[j]
        out = getattr(r, "grad_w_" + kind)
        if kind in ("down", "dense"):
            dst = out.at[pl.ds(k * W, W), :]
        else:
            dst = out.at[:, pl.ds(k * W, W)]
        return pltpu.make_async_copy(mine.at[n, z], dst, r.out_sem.at[j])

    def finish(j):
        mine, into, end, n = slots[j]

        @pl.when(z > 0)
        def _():
            up(j, z).wait_recv()
            mine[n, z] = mine[n, z] + into[n, z]

        @pl.when(z < 3)
        def _():
            down(j, z, True).wait_recv()
            mine[n, z] = mine[n, z] + end[n]

        result_copy(j).start()

    def advance(j):
        if j < len(chunks):
            product(j)
        for lag, step in ((RELAY, relay), (AGAIN, relay_again), (FINISH, finish)):
            if 0 <= j - lag < len(chunks):
                step(j - lag)

    r.acc[...] = jnp.zeros_like(r.acc)
    loads["tok"].wait()

    def first_norm(i):
        at = rows_at(i, 32)
        values = r.tok[at, :].astype(f32)
        average = jnp.mean(values, axis=-1, keepdims=True)
        centered = values - average
        inverse = lax.rsqrt(jnp.mean(centered * centered, axis=-1, keepdims=True) + EPSILON)
        r.average1[at, :] = average
        r.inverse1[at, :] = inverse
        r.first_in[at, :] = (centered * inverse * r.gain1[...] + r.shift1[...]).astype(bf16)

    loop(rows // 32, first_norm)
    loads["w_qkv_v"].wait()

    for n in range(n_q):
        at = slice(n * W, (n + 1) * W)
        value = contract(r.first_in[...], r.w_qkv_v[:, at], 1, 0)
        bias = jnp.concatenate(
            [r.bias_qkv[i : i + 1] for i in range(n * W // B, (n + 1) * W // B)], axis=1
        )
        r.joined[:, at] = (value + bias).astype(bf16)

    seg_row = r.seg_row[...].astype(f32)
    r.seg_col[...] = jnp.broadcast_to(seg_row, (8, rows)).T[:, :1]
    for i in range(rows // B):
        at, ends = slice(i * B, (i + 1) * B), (i + 1) * B
        here = lax.broadcasted_iota(jnp.int32, (B, ends), 0) + i * B
        there = lax.broadcasted_iota(jnp.int32, (B, ends), 1)
        allowed = (r.seg_col[at, :] == seg_row[:, :ends]) & (there <= here)
        r.part_m[at, :ends] = jnp.where(allowed, (there - here).astype(f32), -1e34)
    pl.semaphore_wait(barrier, 9)
    loads["cot"].wait()
    start_block(COT, r.cot)
    start_block(FI, r.first_in)

    for h in range(heads):
        start = 3 * h * HD
        power = (seat * heads + h + 1).astype(f32) * (-8.0 / H)
        slope = jnp.exp2(jnp.full((1, rows), power, f32))
        for i in range(rows // B):
            at, ends = slice(i * B, (i + 1) * B), (i + 1) * B
            raw = contract(
                r.joined[at, start : start + HD], r.joined[:ends, start + HD : start + 2 * HD], 1, 1
            )
            scores = raw * scaling + slope[:, :ends] * r.part_m[at, :ends]
            weights = jnp.exp(scores - jnp.max(scores, axis=-1, keepdims=True))
            prob = weights * (1.0 / jnp.sum(weights, axis=-1, keepdims=True))
            r.probs[h, at, :ends] = prob
            if ends < rows:
                r.probs[h, at, ends:] = jnp.zeros((B, rows - ends), f32)
            value = contract(
                prob.astype(bf16), r.joined[:ends, start + 2 * HD : start + 3 * HD], 1, 0
            ).astype(bf16)
            r.ctx_b[at, h * HD : (h + 1) * HD] = value
    r.ctx_s[...] = r.ctx_b[...].astype(f32)
    ctx_send().start()
    loads["w_dense_v"].wait()
    make_partial(ATT, lambda at, n: contract(r.ctx_b[at, :], r.w_dense_v[:, rows_at(n, W)], 1, 0))
    open_sum(ATT)

    loads["w_down_v"].wait()

    def early(k):
        at = rows_at(k, W)
        r.broad[:, at] = contract(r.cot[...], r.w_down_v[at, :], 1, 1)

    loop(n_u, early)
    loop(rows // 16, lambda i: gather(BDOWN, r.cot[rows_at(i, 16), :].astype(f32)))
    pass_block(COT)
    pass_block(FI)
    for t in range(4):
        r.right[:rows, t * B : (t + 1) * B] = r.cot[:, column(t, x)]
        r.left_q[t * B : (t + 1) * B, :rows] = (
            r.first_in[:, column(t, x)].astype(f32).T.astype(bf16)
        )
    def second_norm(start):
        def body(i):
            at = pl.ds(pl.multiple_of(start + i * 16, 16), 16)
            values = r.tok[at, :].astype(f32) + r.sum_a[at, :] + r.bias_dense[...]
            average = jnp.mean(values, axis=-1, keepdims=True)
            centered = values - average
            inverse = lax.rsqrt(jnp.mean(centered * centered, axis=-1, keepdims=True) + EPSILON)
            r.hidden[at, :] = values
            r.average2[at, :] = average
            r.inverse2[at, :] = inverse
            r.second_in[at, :] = (centered * inverse * r.gain2[...] + r.shift2[...]).astype(bf16)

        loop(sub // 16, body)

    close_all(ATT, second_norm)

    loads["w_up_v"].wait()
    for k in range(n_u):
        columns = slice(k * W, (k + 1) * W)
        r.act_s[k] = contract(r.second_in[...], r.w_up_v[:, columns], 1, 0) + r.bias_up[:, columns]

        def gelu_step(i, k=k, columns=columns):
            at = rows_at(i, 32)
            value, slope = gelu_pair(r.act_s[k, at, :])
            r.act_s[k, at, :] = value
            r.act_b[k, at, :] = value.astype(bf16)
            change = r.broad[at, columns] * slope
            r.gu_s[k, at, :] = change
            r.gu_b[k, at, :] = change.astype(bf16)
            gather(BUP, change, columns)

        loop(rows // 32, gelu_step)
        act_send(k).start()
    blk_send(COT).wait_send()
    start_block(SI, r.second_in)
    for k in range(n_u):
        gu_send(k).start()

    def up_terms(at, n):
        return sum(
            contract(r.gu_b[k, at, :], r.w_up_v[rows_at(n, W), k * W : (k + 1) * W], 1, 1)
            for k in range(n_u)
        )

    def mixed_terms(at, n):
        return sum(
            contract(r.act_b[k, at, :], r.w_down_v[k * W : (k + 1) * W, rows_at(n, W)], 1, 0)
            for k in range(n_u)
        )

    for k in range(CHUNKS):
        near_copy(ATT, k).wait_send()
    make_partial(GN2, up_terms)
    for k in range(CHUNKS):
        back_copy(ATT, k).wait_send()
    open_sum(GN2)
    make_partial(MIX, mixed_terms)
    open_sum(MIX)
    for t in range(4):
        r.left_u[t * B : (t + 1) * B, :rows] = (
            r.second_in[:, column(t, x)].astype(f32).T.astype(bf16)
        )
    take_block(COT)
    take_block(FI)
    for t in range(4):
        r.right[rows:, t * B : (t + 1) * B] = r.blk_r[COT, t].astype(bf16)
        r.left_q[t * B : (t + 1) * B, rows:] = r.blk_r[FI, t].T.astype(bf16)
    advance(0)
    advance(1)

    def hidden_step(start):
        def body(i):
            at = pl.ds(pl.multiple_of(start + i * 16, 16), 16)
            upstream = r.sum_a[at, :]
            normed = (r.hidden[at, :] - r.average2[at, :]) * r.inverse2[at, :]
            change = norm_backward(upstream, normed, r.inverse2[at, :], r.gain2[...])
            value = r.cot[at, :].astype(f32) + change
            r.broad[at, :] = value
            r.gh_b[at, :] = value.astype(bf16)
            gather(GAIN2, upstream * normed)
            gather(SHIFT2, upstream)
            gather(BDENSE, value)

        loop(sub // 16, body)

    close_all(GN2, hidden_step)
    blk_send(FI).wait_send()
    start_block(GH, r.gh_b)
    r.gctx[...] = contract(r.gh_b[...], r.w_dense_v[...], 1, 1).astype(bf16)
    advance(2)

    for h in range(heads):
        start = 3 * h * HD
        queries = r.joined[:, start : start + HD]
        key_vecs = r.joined[:, start + HD : start + 2 * HD]
        val_vecs = r.joined[:, start + 2 * HD : start + 3 * HD]
        upstream = r.gctx[:, h * HD : (h + 1) * HD]
        prob = r.probs[h]
        grad_probs = contract(upstream, val_vecs, 1, 1)
        row_inner = jnp.sum(prob * grad_probs, axis=-1, keepdims=True)
        grad_scores = (prob * (grad_probs - row_inner)).astype(bf16)
        thirds = (
            contract(grad_scores, key_vecs, 1, 0) * scaling,
            contract(grad_scores, queries, 0, 0) * scaling,
            contract(prob.astype(bf16), upstream, 0, 0),
        )
        for third, value in enumerate(thirds):
            k, offset = divmod(start + third * HD, W)
            r.gj_s[k, :, offset : offset + HD] = value
    for k in range(n_q):
        gj_send(k).start()

        def joined_grad(i, k=k):
            at = rows_at(i, 32)
            value = r.gj_s[k, at, :]
            r.gj_b[k, at, :] = value.astype(bf16)
            gather(BQKV, value, slice(k * W, (k + 1) * W))

        loop(rows // 32, joined_grad)

    def joined_terms(at, n):
        return sum(
            contract(r.gj_b[k, at, :], r.w_qkv_v[rows_at(n, W), k * W : (k + 1) * W], 1, 1)
            for k in range(n_q)
        )

    for k in range(CHUNKS):
        near_copy(GN2, k).wait_send()
        back_copy(GN2, k).wait_send()
    make_partial(GN1, joined_terms)
    open_sum(GN1)
    advance(3)

    pass_block(SI)
    take_block(SI)
    for t in range(4):
        r.left_u[t * B : (t + 1) * B, rows:] = r.blk_r[SI, t].T.astype(bf16)

    def output_step(start):
        def body(i):
            at = pl.ds(pl.multiple_of(start + i * 16, 16), 16)
            value = r.hidden[at, :] + r.sum_m[at, :] + r.bias_down[...]
            r.second_in[at, :] = value.astype(bf16)

        loop(sub // 16, body)

    close_all(MIX, output_step)
    output_copy = pltpu.make_async_copy(r.second_in, r.output, r.load_sem.at[0])
    output_copy.start()
    advance(4)
    advance(5)

    def input_step(start):
        def body(i):
            at = pl.ds(pl.multiple_of(start + i * 16, 16), 16)
            upstream = r.sum_a[at, :]
            inverse = r.inverse1[at, :]
            normed = (r.tok[at, :].astype(f32) - r.average1[at, :]) * inverse
            change = norm_backward(upstream, normed, inverse, r.gain1[...])
            gather(GAIN1, upstream * normed)
            gather(SHIFT1, upstream)
            r.broad[at, :] = r.broad[at, :] + change

        loop(sub // 16, body)

    close_all(GN1, input_step)
    input_copy = pltpu.make_async_copy(r.broad, r.grad_input, r.load_sem.at[1])
    input_copy.start()

    for v in range(8):
        vector = jnp.sum(r.acc[v], axis=0, keepdims=True)
        if v == BQKV:
            piece = n_q * W // 8
        else:
            piece = B
        for p in range(8):
            r.table[p, v : v + 1, :piece] = vector[:, p * piece : (p + 1) * piece]

    def vector_send(step):
        peer = (place + step) % 8
        return send(
            r.table.at[peer], r.vec_r.at[step], r.vs.at[step], r.vr.at[step], {"dp": peer}
        )

    for step in range(1, 8):
        vector_send(step).start()
    advance(6)
    advance(7)
    pass_block(GH)
    for t in range(4):
        r.right[:rows, t * B : (t + 1) * B] = r.gh_b[:, column(t, x)]
    take_block(GH)
    for t in range(4):
        r.right[rows:, t * B : (t + 1) * B] = r.blk_r[GH, t].astype(bf16)
    ctx_send().wait_recv()
    advance(8)
    vector = r.table[place]
    for step in range(1, 8):
        vector_send(step).wait_recv()
        vector = vector + r.vec_r[step]
    r.vectors[...] = vector
    for j in range(9, len(chunks) + FINISH):
        advance(j)

    for k in range(n_u):
        act_send(k).wait_send()
        gu_send(k).wait_send()
    for k in range(n_q):
        gj_send(k).wait_send()
    ctx_send().wait_send()
    for n in range(4):
        if n in (SI, GH):
            blk_send(n).wait_send()
        for i in range(3):
            blk_pass(n, i).wait_send()
    for a in range(SUMS):
        for k in range(CHUNKS):
            if a in (MIX, GN1):
                near_copy(a, k).wait_send()
                back_copy(a, k).wait_send()
            far_copy(a, k).wait_send()
    for step in range(1, 8):
        vector_send(step).wait_send()
    for j in range(len(chunks)):
        for t in range(4):

            @pl.when(z < t)
            def _():
                up(j, t).wait_send()

            @pl.when(z > t)
            def _():
                down(j, t, False).wait_send()

        result_copy(j).wait()
    output_copy.wait()
    input_copy.wait()


def deliver_kernel(count, *refs):
    sources, vectors = refs[:count], refs[count]
    results, parts = refs[count + 1 : 2 * count + 1], refs[2 * count + 1 : 2 * count + 9]
    held, load_sem, store_sem = refs[2 * count + 9 : 3 * count + 9], refs[-2], refs[-1]
    loads = [
        pltpu.make_async_copy(src, mid, load_sem.at[i])
        for i, (src, mid) in enumerate(zip(sources, held))
    ]
    stores = [
        pltpu.make_async_copy(mid, dst, store_sem.at[i])
        for i, (mid, dst) in enumerate(zip(held, results))
    ]
    for copy in loads:
        copy.start()
    for v, part in enumerate(parts):
        part[...] = vectors[v : v + 1, : part.shape[1]]
    for load, store in zip(loads, stores):
        load.wait()
        store.start()
    for store in stores:
        store.wait()


def whole_layer(tokens, segment_ids, cotangent, *rest):
    (
        norm1_gain,
        norm1_shift,
        w_qkv,
        b_qkv,
        w_dense,
        b_dense,
        norm2_gain,
        norm2_shift,
        w_up,
        b_up,
        w_down,
        b_down,
    ) = rest
    rows, width = tokens.shape
    joined = w_qkv.shape[1]
    heads = joined // (3 * HD)
    inner = heads * HD
    units = w_up.shape[1]
    n_u, n_q = units // W, joined // W
    n_wide = n_u + n_q
    n_all = N_TALL + n_wide
    sub = rows // 2 // CHUNKS
    inputs = [
        ("seg_row", segment_ids),
        ("gain1", norm1_gain[None]),
        ("shift1", norm1_shift[None]),
        ("bias_qkv", b_qkv.reshape(-1, B)),
        ("bias_dense", b_dense[None]),
        ("gain2", norm2_gain[None]),
        ("shift2", norm2_shift[None]),
        ("bias_up", b_up[None]),
        ("bias_down", b_down[None]),
        ("tokens", tokens),
        ("cotangent", cotangent),
        ("w_qkv", w_qkv),
        ("w_dense", w_dense),
        ("w_up", w_up),
        ("w_down", w_down),
    ]
    small = 9
    outs = [
        ("output", (rows, width), bf16),
        ("grad_input", (rows, width), f32),
        ("grad_w_qkv", (width // 8, joined), f32),
        ("grad_w_dense", (inner, width // 8), f32),
        ("grad_w_up", (width // 8, units), f32),
        ("grad_w_down", (units, width // 8), f32),
        ("vectors", (8, B), f32),
    ]
    dma = pltpu.SemaphoreType.DMA
    scratch = [
        ("tok", (rows, width), bf16),
        ("cot", (rows, width), bf16),
        ("w_qkv_v", w_qkv.shape, bf16),
        ("w_dense_v", w_dense.shape, bf16),
        ("w_up_v", w_up.shape, bf16),
        ("w_down_v", w_down.shape, bf16),
        ("seg_col", (rows, 1), f32),
        ("average1", (rows, 1), f32),
        ("inverse1", (rows, 1), f32),
        ("average2", (rows, 1), f32),
        ("inverse2", (rows, 1), f32),
        ("first_in", (rows, width), bf16),
        ("second_in", (rows, width), bf16),
        ("hidden", (rows, width), f32),
        ("broad", (rows, width), f32),
        ("gh_b", (rows, width), bf16),
        ("joined", (rows, joined), bf16),
        ("probs", (heads, rows, rows), f32),
        ("ctx_b", (rows, inner), bf16),
        ("gctx", (rows, inner), bf16),
        ("act_b", (n_u, rows, W), bf16),
        ("gu_b", (n_u, rows, W), bf16),
        ("gj_b", (n_q, rows, W), bf16),
        ("act_s", (n_u, rows, W), f32),
        ("act_r", (n_u, rows, W), f32),
        ("gu_s", (n_u, rows, W), f32),
        ("gu_r", (n_u, rows, W), f32),
        ("gj_s", (n_q, rows, W), f32),
        ("gj_r", (n_q, rows, W), f32),
        ("ctx_s", (rows, inner), f32),
        ("ctx_r", (rows, inner), f32),
        ("blk_s", (2, rows, B), f32),
        ("blk_r", (4, 4, rows, B), f32),
        ("right", (2 * rows, 4 * B), bf16),
        ("left_u", (4 * B, 2 * rows), bf16),
        ("left_q", (4 * B, 2 * rows), bf16),
        ("part_a", (rows, width), f32),
        ("part_m", (rows, width), f32),
        ("sum_a", (rows, width), f32),
        ("sum_m", (rows, width), f32),
        ("near", (SUMS, CHUNKS, sub, width), f32),
        ("far", (SUMS, CHUNKS, sub, width), f32),
        ("own_t", (N_TALL, 4, W, B), f32),
        ("in_t", (N_TALL, 4, W, B), f32),
        ("end_t", (N_TALL, W, B), f32),
        ("own_w", (n_wide, 4, B, W), f32),
        ("in_w", (n_wide, 4, B, W), f32),
        ("end_w", (n_wide, B, W), f32),
        ("acc", (8, 8, width), f32),
        ("table", (8, 8, B), f32),
        ("vec_r", (8, 8, B), f32),
    ]
    sems = [
        ("load_sem", (6,)),
        ("out_sem", (n_all,)),
        ("act_ss", (n_u,)),
        ("act_rs", (n_u,)),
        ("gu_ss", (n_u,)),
        ("gu_rs", (n_u,)),
        ("gj_ss", (n_q,)),
        ("gj_rs", (n_q,)),
        ("ctx_ss", None),
        ("ctx_rs", None),
        ("bs", (4,)),
        ("br", (4,)),
        ("fs", (4, 3)),
        ("fr", (4, 3)),
        ("cs", (SUMS, CHUNKS)),
        ("cr", (SUMS, CHUNKS)),
        ("ys", (SUMS, CHUNKS)),
        ("yr", (SUMS, CHUNKS)),
        ("ks", (SUMS, CHUNKS)),
        ("kr", (SUMS, CHUNKS)),
        ("us", (n_all, 4)),
        ("ur", (n_all, 4)),
        ("ds", (n_all, 4)),
        ("dr", (n_all, 4)),
        ("vs", (8,)),
        ("vr", (8,)),
    ]
    names = [n for n, _ in inputs] + [o[0] for o in outs] + [s[0] for s in scratch]
    names += [n for n, _ in sems]
    vmem, anywhere = pl.BlockSpec(memory_space=pltpu.VMEM), pl.BlockSpec(memory_space=pl.ANY)
    results = pl.pallas_call(
        functools.partial(layer_kernel, names),
        out_shape=[jax.ShapeDtypeStruct(shape, kind) for _, shape, kind in outs],
        in_specs=[vmem] * small + [anywhere] * (len(inputs) - small),
        out_specs=[anywhere] * (len(outs) - 1) + [vmem],
        scratch_shapes=[pltpu.VMEM(shape, kind) for _, shape, kind in scratch]
        + [dma(shape) if shape else dma for _, shape in sems],
        compiler_params=pltpu.CompilerParams(
            collective_id=7, has_side_effects=True, vmem_limit_bytes=63 * MIB
        ),
    )(*[value for _, value in inputs])
    lengths = [joined // 8 if v == BQKV else B for v in range(8)]
    results = pl.pallas_call(
        functools.partial(deliver_kernel, len(outs) - 1),
        out_shape=[jax.ShapeDtypeStruct(o.shape, o.dtype) for o in results[:-1]]
        + [jax.ShapeDtypeStruct((1, n), f32) for n in lengths],
        in_specs=[anywhere] * (len(outs) - 1) + [vmem],
        out_specs=[anywhere] * (len(outs) - 1) + [vmem] * 8,
        scratch_shapes=[pltpu.VMEM(o.shape, o.dtype) for o in results[:-1]]
        + [dma((len(outs) - 1,))] * 2,
    )(*results)
    output, grad_input, g_qkv, g_dense, g_up, g_down = results[: len(outs) - 1]
    v = [o.reshape(-1) for o in results[len(outs) - 1 :]]
    return (
        output,
        grad_input,
        v[GAIN1],
        v[SHIFT1],
        g_qkv,
        v[BQKV],
        g_dense,
        v[BDENSE],
        v[GAIN2],
        v[SHIFT2],
        g_up,
        v[BUP],
        g_down,
        v[BDOWN],
    )


def solution(mesh):
    in_specs = (
        P("dp", None),
        P("dp", None),
        P("dp", None),
        P(),
        P(),
        P(None, "tensor"),
        P("tensor"),
        P("tensor", None),
        P(),
        P(),
        P(),
        P(None, "tensor"),
        P("tensor"),
        P("tensor", None),
        P(),
    )
    out_specs = (
        P("dp", None),
        P("dp", None),
        P("dp"),
        P("dp"),
        P("dp", "tensor"),
        P(("tensor", "dp")),
        P("tensor", "dp"),
        P("dp"),
        P("dp"),
        P("dp"),
        P("dp", "tensor"),
        P(("tensor", "dp")),
        P("tensor", "dp"),
        P("dp"),
    )
    sizes = (mesh.shape["dp"], mesh.shape["tensor"])
    body = whole_layer if sizes == (8, 4) else functools.partial(local, sizes)
    return jax.shard_map(body, mesh=mesh, in_specs=in_specs, out_specs=out_specs, check_vma=False)
```

```python
import functools
import math
from types import SimpleNamespace

import jax
import jax.numpy as jnp
from jax import lax
from jax.experimental import pallas as pl
from jax.experimental.pallas import tpu as pltpu
from jax.sharding import PartitionSpec as P

H = 16
HD = 64


EPSILON = 1e-05
GELU_COEF = math.sqrt(2.0 / math.pi)


def layer_norm(values, gain, shift):
    average = jnp.mean(values, axis=-1, keepdims=True)
    centered = values - average
    variance = jnp.mean(centered * centered, axis=-1, keepdims=True)
    inverse = lax.rsqrt(variance + EPSILON)
    normed = centered * inverse
    return (normed * gain + shift, normed, inverse)


def norm_backward(upstream, normed, inverse, gain):
    scaled = upstream * gain
    return inverse * (
        scaled
        - jnp.mean(scaled, axis=-1, keepdims=True)
        - normed * jnp.mean(scaled * normed, axis=-1, keepdims=True)
    )


def gelu_pair(inputs):
    tangent = jnp.tanh(GELU_COEF * (inputs + 0.044715 * inputs * inputs * inputs))
    result = 0.5 * inputs * (1.0 + tangent)
    derivative = 0.5 * (1.0 + tangent) + 0.5 * inputs * (1.0 - tangent * tangent) * GELU_COEF * (
        1.0 + 3.0 * 0.044715 * inputs * inputs
    )
    return (result, derivative)


def head_scores(queries, key_vecs, slopes, offset, allowed, scaling):
    raw_scores = jnp.einsum("ihe,jhe->hij", queries, key_vecs, preferred_element_type=jnp.float32)
    return jnp.where(
        allowed[None], raw_scores * scaling + slopes[:, None, None] * offset[None], -1e30
    )

CHUNKS = 4
MESH = pl.DeviceIdType.MESH
MIB = 1024 * 1024


def scatter(grads, kinds):
    return [
        lax.psum_scatter(g, "dp", scatter_dimension=0 if k == "rows" else 1, tiled=True)
        for g, k in zip(grads, kinds)
    ]


def scatter_vectors(vectors, n_dp):
    widths = [v.shape[0] // n_dp for v in vectors]
    widest = -(-max(widths) // 128) * 128
    table = jnp.stack(
        [jnp.pad(v.reshape(n_dp, -1), ((0, 0), (0, widest - w))) for v, w in zip(vectors, widths)],
        axis=1,
    ).reshape(n_dp * len(vectors), widest)
    (mine,) = scatter([table], ["rows"])
    return [mine[i, :w] for i, w in enumerate(widths)]


def local(
    sizes,
    tokens,
    segment_ids,
    cotangent,
    norm1_gain,
    norm1_shift,
    w_qkv,
    b_qkv,
    w_dense,
    b_dense,
    norm2_gain,
    norm2_shift,
    w_up,
    b_up,
    w_down,
    b_down,
):
    segments = segment_ids[0]
    row_count = tokens.shape[0]
    heads_here = w_qkv.shape[1] // (3 * HD)
    head_start = lax.axis_index("tensor") * heads_here
    scaling = 1.0 / math.sqrt(HD)
    slopes = 2.0 ** (-8.0 * (head_start + jnp.arange(heads_here) + 1).astype(jnp.float32) / H)
    places = jnp.arange(row_count)
    offset = (places[None, :] - places[:, None]).astype(jnp.float32)
    allowed = (segments[:, None] == segments[None, :]) & (places[None, :] <= places[:, None])
    inputs = tokens.astype(jnp.float32)
    first_out, normed1, inverse1 = layer_norm(inputs, norm1_gain, norm1_shift)
    first_in = first_out.astype(jnp.bfloat16)
    joined = (jnp.dot(first_in, w_qkv, preferred_element_type=jnp.float32) + b_qkv).astype(
        jnp.bfloat16
    )
    joined = joined.reshape(row_count, heads_here, 3, HD)
    queries = joined[:, :, 0]
    key_vecs = joined[:, :, 1]
    val_vecs = joined[:, :, 2]
    scores = head_scores(queries, key_vecs, slopes, offset, allowed, scaling)
    highest = jnp.max(scores, axis=-1, keepdims=True)
    log_total = highest + jnp.log(jnp.sum(jnp.exp(scores - highest), axis=-1, keepdims=True))
    probs = jnp.exp(scores - log_total)
    probs_b = probs.astype(jnp.bfloat16)
    context = jnp.einsum(
        "hij,jhe->ihe", probs_b, val_vecs, preferred_element_type=jnp.float32
    ).astype(jnp.bfloat16)
    context = context.reshape(row_count, heads_here * HD)
    attended = lax.psum(jnp.dot(context, w_dense, preferred_element_type=jnp.float32), "tensor")
    hidden = inputs + attended + b_dense
    second_out, normed2, inverse2 = layer_norm(hidden, norm2_gain, norm2_shift)
    second_in = second_out.astype(jnp.bfloat16)
    upward = jnp.dot(second_in, w_up, preferred_element_type=jnp.float32) + b_up
    activated, gelu_slope = gelu_pair(upward)
    activated_b = activated.astype(jnp.bfloat16)
    mixed = jnp.dot(activated_b, w_down, preferred_element_type=jnp.float32)
    grad_out = cotangent.astype(jnp.float32)
    grad_w_down = jnp.dot(activated_b.T, cotangent, preferred_element_type=jnp.float32)
    grad_b_down = jnp.sum(grad_out, axis=0)
    grad_up = jnp.dot(cotangent, w_down.T, preferred_element_type=jnp.float32) * gelu_slope
    grad_up_b = grad_up.astype(jnp.bfloat16)
    grad_w_up = jnp.dot(second_in.T, grad_up_b, preferred_element_type=jnp.float32)
    grad_b_up = jnp.sum(grad_up, axis=0)
    grad_norm2 = jnp.dot(grad_up_b, w_up.T, preferred_element_type=jnp.float32)
    grad_norm2 = lax.psum(grad_norm2, "tensor")
    mixed = lax.psum(mixed, "tensor")
    grad_hidden = grad_out + norm_backward(grad_norm2, normed2, inverse2, norm2_gain)
    grad_hidden_b = grad_hidden.astype(jnp.bfloat16)
    grad_w_dense = jnp.dot(context.T, grad_hidden_b, preferred_element_type=jnp.float32)
    grad_context = jnp.dot(grad_hidden_b, w_dense.T, preferred_element_type=jnp.float32).astype(
        jnp.bfloat16
    )
    grad_context = grad_context.reshape(row_count, heads_here, HD)
    scores_again = head_scores(queries, key_vecs, slopes, offset, allowed, scaling)
    probs_again = jnp.exp(scores_again - log_total)
    probs_again_b = probs_again.astype(jnp.bfloat16)
    grad_vals = jnp.einsum(
        "hij,ihe->jhe", probs_again_b, grad_context, preferred_element_type=jnp.float32
    )
    grad_probs = jnp.einsum(
        "ihe,jhe->hij", grad_context, val_vecs, preferred_element_type=jnp.float32
    )
    row_inner = jnp.sum(probs_again * grad_probs, axis=-1, keepdims=True)
    grad_scores = (probs_again * (grad_probs - row_inner)).astype(jnp.bfloat16)
    grad_queries = (
        jnp.einsum("hij,jhe->ihe", grad_scores, key_vecs, preferred_element_type=jnp.float32)
        * scaling
    )
    grad_keys = (
        jnp.einsum("hij,ihe->jhe", grad_scores, queries, preferred_element_type=jnp.float32)
        * scaling
    )
    grad_joined = jnp.stack([grad_queries, grad_keys, grad_vals], axis=2).reshape(
        row_count, 3 * heads_here * HD
    )
    grad_joined_b = grad_joined.astype(jnp.bfloat16)
    grad_w_qkv = jnp.dot(first_in.T, grad_joined_b, preferred_element_type=jnp.float32)
    grad_norm1 = jnp.dot(grad_joined_b, w_qkv.T, preferred_element_type=jnp.float32)
    grad_norm1 = lax.psum(grad_norm1, "tensor")
    grad_w_up, grad_w_down, grad_w_qkv, grad_w_dense = scatter(
        [grad_w_up, grad_w_down, grad_w_qkv, grad_w_dense],
        ["rows", "columns", "rows", "columns"],
    )
    output = (hidden + mixed + b_down).astype(jnp.bfloat16)
    grad_gain2 = jnp.sum(grad_norm2 * normed2, axis=0)
    grad_shift2 = jnp.sum(grad_norm2, axis=0)
    grad_b_dense = jnp.sum(grad_hidden, axis=0)
    grad_b_qkv = jnp.sum(grad_joined, axis=0)
    grad_gain1 = jnp.sum(grad_norm1 * normed1, axis=0)
    grad_shift1 = jnp.sum(grad_norm1, axis=0)
    grad_input = grad_hidden + norm_backward(grad_norm1, normed1, inverse1, norm1_gain)
    vectors = scatter_vectors(
        [
            grad_gain1,
            grad_shift1,
            grad_b_qkv,
            grad_b_dense,
            grad_gain2,
            grad_shift2,
            grad_b_up,
            grad_b_down,
        ],
        sizes[0],
    )
    gain1, shift1, b_qkv_part, b_dense_part, gain2, shift2, b_up_part, b_down_part = vectors
    return (
        output,
        grad_input,
        gain1,
        shift1,
        grad_w_qkv,
        b_qkv_part,
        grad_w_dense,
        b_dense_part,
        gain2,
        shift2,
        grad_w_up,
        b_up_part,
        grad_w_down,
        b_down_part,
    )


W = 256
B = 128
SUMS = 4
ATT, GN2, MIX, GN1 = range(SUMS)
COT, FI, SI, GH = range(4)
GAIN1, SHIFT1, BQKV, BDENSE, GAIN2, SHIFT2, BUP, BDOWN = range(8)
N_TALL = 5
RELAY, AGAIN, FINISH = 1, 2, 4
f32 = jnp.float32
bf16 = jnp.bfloat16


def contract(left, right, left_axis, right_axis):
    return lax.dot_general(
        left, right, (((left_axis,), (right_axis,)), ((), ())), preferred_element_type=f32
    )


def loop(count, body):
    def step(i, carry):
        body(i)
        return carry

    lax.fori_loop(0, count, step, 0)


def rows_at(i, size):
    return pl.ds(pl.multiple_of(i * size, size), size)


def layer_kernel(names, items, *refs):
    r = SimpleNamespace(**dict(zip(names, refs)))
    rows, width = r.tok.shape
    half = rows // 2
    sub = half // CHUNKS
    heads = r.probs.shape[0]
    units = r.w_up_v.shape[1]
    n_u = units // W
    n_q = r.w_qkv_v.shape[1] // W
    scaling = 1.0 / math.sqrt(HD)
    place, seat = lax.axis_index("dp"), lax.axis_index("tensor")
    z, x = place // 2, place % 2
    y, core = seat // 2, seat % 2
    other_x = {"dp": z * 2 + 1 - x}
    above, below = {"dp": place + 2}, {"dp": place - 2}
    other_core = {"tensor": y * 2 + 1 - core}
    other_y = {"tensor": (1 - y) * 2 + core}

    loads = {}
    pairs = [
        ("tok", "tokens"),
        ("w_qkv_v", "w_qkv"),
        ("cot", "cotangent"),
        ("w_dense_v", "w_dense"),
        ("w_down_v", "w_down"),
        ("w_up_v", "w_up"),
    ]
    for i, (dst, src) in enumerate(pairs):
        loads[dst] = pltpu.make_async_copy(getattr(r, src), getattr(r, dst), r.load_sem.at[i])
        loads[dst].start()

    barrier = pltpu.get_barrier_semaphore()
    for step in range(1, 8):
        peer = {"dp": (place + step) % 8}
        pl.semaphore_signal(barrier, inc=1, device_id=peer, device_id_type=MESH)
    pl.semaphore_signal(barrier, inc=1, device_id=other_core, device_id_type=MESH)
    pl.semaphore_signal(barrier, inc=1, device_id=other_y, device_id_type=MESH)

    def send(src, dst, send_sem, recv_sem, device):
        return pltpu.make_async_remote_copy(
            src_ref=src,
            dst_ref=dst,
            send_sem=send_sem,
            recv_sem=recv_sem,
            device_id=device,
            device_id_type=MESH,
        )

    def x_send(j):
        kind, k, lo, size = items[j]
        out, into = {"down": (r.act_s, r.act_r), "up": (r.gu_s, r.gu_r), "qkv": (r.gj_s, r.gj_r)}[
            kind
        ]
        at = (k, slice(None), pl.ds(lo, size))
        return send(out.at[at], into.at[at], r.xs.at[j], r.xr.at[j], other_x)

    def start_items(kind, ks):
        for j, item in enumerate(items):
            if item[0] == kind and item[1] in ks:
                x_send(j).start()

    def ctx_send():
        return send(r.ctx_s, r.ctx_r, r.ctx_ss, r.ctx_rs, other_x)

    def blk_send(n):
        return send(r.blk_s.at[n % 2], r.blk_r.at[n, seat], r.bs.at[n], r.br.at[n], other_x)

    def blk_pass(n, i):
        part = r.blk_r.at[n, (seat if i < 2 else 2 * (1 - y) + core)]
        device = other_y if i == 1 else other_core
        return send(part, part, r.fs.at[n, i], r.fr.at[n, i], device)

    def column(t, side):
        return pl.ds(pl.multiple_of((2 * t + side) * B, B), B)

    def start_block(n, source):
        r.blk_s[n % 2] = source[:, column(seat, 1 - x)].astype(f32)
        blk_send(n).start()

    def pass_block(n):
        blk_send(n).wait_recv()
        blk_pass(n, 0).start()
        blk_pass(n, 1).start()

    def take_block(n):
        blk_pass(n, 1).wait_recv()
        blk_pass(n, 2).start()
        blk_pass(n, 0).wait_recv()
        blk_pass(n, 2).wait_recv()

    def partial(a):
        return r.part_m if a == MIX else r.part_a

    def total(a):
        return r.sum_m if a == MIX else r.sum_a

    def own(k):
        return pl.ds(pl.multiple_of(core * half + k * sub, sub), sub)

    def its(k):
        return pl.ds(pl.multiple_of((1 - core) * half + k * sub, sub), sub)

    def near_copy(a, k):
        return send(
            partial(a).at[its(k), :], r.near.at[a, k], r.cs.at[a, k], r.cr.at[a, k], other_core
        )

    def far_copy(a, k):
        return send(r.near.at[a, k], r.far.at[a, k], r.ys.at[a, k], r.yr.at[a, k], other_y)

    def back_copy(a, k):
        part = total(a).at[own(k), :]
        return send(part, part, r.ks.at[a, k], r.kr.at[a, k], other_core)

    def make_partial(a, terms):
        dst = partial(a)
        for side in (1, 0):
            start = pl.multiple_of((core if side == 0 else 1 - core) * half, half)
            at = pl.ds(start, half)
            loop(width // W, lambda n: dst.__setitem__((at, rows_at(n, W)), terms(at, n)))
            if side:
                for k in range(CHUNKS):
                    near_copy(a, k).start()

    def open_sum(a):
        for k in range(CHUNKS):
            near_copy(a, k).wait_recv()
            r.near[a, k] = r.near[a, k] + partial(a)[own(k), :]
            far_copy(a, k).start()

    def close_sum(a, k):
        far_copy(a, k).wait_recv()
        total(a)[own(k), :] = r.near[a, k] + r.far[a, k]
        back_copy(a, k).start()

    def close_all(a, work):
        for k in range(CHUNKS):
            close_sum(a, k)
            work(core * half + k * sub)
            if k:
                back_copy(a, k - 1).wait_recv()
                work((1 - core) * half + (k - 1) * sub)
        back_copy(a, CHUNKS - 1).wait_recv()
        work((1 - core) * half + (CHUNKS - 1) * sub)

    def gather(v, values, at=None):
        part = values[0:8]
        for i in range(1, values.shape[0] // 8):
            part = part + values[8 * i : 8 * i + 8]
        if at is None:
            r.acc[v] = r.acc[v] + part
        else:
            r.acc[v, :, at] = r.acc[v, :, at] + part

    slots, n_tall, n_wide = [], 0, 0
    for kind, _, lo, size in items:
        if kind in ("down", "dense"):
            slots.append((r.own_t, r.in_t, r.end_t, n_tall))
            n_tall += lo + size == W
        else:
            slots.append((r.own_w, r.in_w, r.end_w, n_wide))
            n_wide += lo + size == W

    def view(ref, j, *at):
        kind, _, lo, size = items[j]
        rest = (pl.ds(lo, size),) if kind in ("down", "dense") else (slice(None), pl.ds(lo, size))
        return ref.at[(slots[j][3], *at, *rest)]

    def up(j, t):
        mine, into, _, _ = slots[j]
        return send(view(mine, j, t), view(into, j, t), r.us.at[j, t], r.ur.at[j, t], above)

    def down(j, t, last):
        mine, into, end, _ = slots[j]
        dst = view(end, j) if last else view(into, j, t)
        return send(view(mine, j, t), dst, r.ds.at[j, t], r.dr.at[j, t], below)

    def product(j):
        kind, k, lo, size = items[j]
        mine = slots[j][0]
        at = slice(lo, lo + size)
        if kind != "dense":
            x_send(j).wait_recv()
        if kind == "down":
            value = contract(r.act_b[k, :, at], r.right[:rows], 0, 0) + contract(
                r.act_r[k, :, at].astype(bf16), r.right[rows:], 0, 0
            )
        elif kind == "dense":
            value = contract(r.ctx_b[...], r.right[:rows], 0, 0) + contract(
                r.ctx_r[...].astype(bf16), r.right[rows:], 0, 0
            )
        else:
            if kind == "up":
                left, here, there = r.left_u, r.gu_b[k, :, at], r.gu_r[k, :, at]
            else:
                left, here, there = r.left_q, r.gj_b[k, :, at], r.gj_r[k, :, at]
            value = contract(left[:, :rows], here, 1, 0) + contract(
                left[:, rows:], there.astype(bf16), 1, 0
            )
        for t in range(4):
            part = slice(t * B, (t + 1) * B)
            view(mine, j, t)[...] = value[:, part] if kind in ("down", "dense") else value[part]

        @pl.when(z == 0)
        def _():
            for t in (3, 2, 1):
                up(j, t).start()

        @pl.when(z == 3)
        def _():
            for t in (0, 1, 2):
                down(j, t, t == 2).start()

    def pass_on(j, t, here, upward):
        mine, into, _, _ = slots[j]

        @pl.when(z == here)
        def _():
            came = up(j, t) if upward else down(j, t, False)
            came.wait_recv()
            view(mine, j, t)[...] = view(mine, j, t)[...] + view(into, j, t)[...]
            onward = up(j, t) if upward else down(j, t, t == here - 1)
            onward.start()

    def relay(j):
        pass_on(j, 3, 1, True)
        pass_on(j, 2, 1, True)
        pass_on(j, 0, 2, False)
        pass_on(j, 1, 2, False)

    def relay_again(j):
        pass_on(j, 3, 2, True)
        pass_on(j, 0, 1, False)

    def result_copy(j):
        kind, k, lo, size = items[j]
        out = getattr(r, "grad_w_" + kind)
        at = pl.ds(k * W + lo, size)
        dst = out.at[at, :] if kind in ("down", "dense") else out.at[:, at]
        return pltpu.make_async_copy(view(slots[j][0], j, z), dst, r.out_sem.at[j])

    def finish(j):
        mine, into, end, _ = slots[j]

        @pl.when(z > 0)
        def _():
            up(j, z).wait_recv()
            view(mine, j, z)[...] = view(mine, j, z)[...] + view(into, j, z)[...]

        @pl.when(z < 3)
        def _():
            down(j, z, True).wait_recv()
            view(mine, j, z)[...] = view(mine, j, z)[...] + view(end, j)[...]

        result_copy(j).start()

    def advance(j):
        if j < len(items):
            product(j)
        for lag, step in ((RELAY, relay), (AGAIN, relay_again), (FINISH, finish)):
            if 0 <= j - lag < len(items):
                step(j - lag)

    r.acc[...] = jnp.zeros_like(r.acc)
    loads["tok"].wait()

    def first_norm(i):
        at = rows_at(i, 32)
        values = r.tok[at, :].astype(f32)
        average = jnp.mean(values, axis=-1, keepdims=True)
        centered = values - average
        inverse = lax.rsqrt(jnp.mean(centered * centered, axis=-1, keepdims=True) + EPSILON)
        r.average1[at, :] = average
        r.inverse1[at, :] = inverse
        r.first_in[at, :] = (centered * inverse * r.gain1[...] + r.shift1[...]).astype(bf16)

    loop(rows // 32, first_norm)
    loads["w_qkv_v"].wait()

    for n in range(n_q):
        at = slice(n * W, (n + 1) * W)
        value = contract(r.first_in[...], r.w_qkv_v[:, at], 1, 0)
        bias = jnp.concatenate(
            [r.bias_qkv[i : i + 1] for i in range(n * W // B, (n + 1) * W // B)], axis=1
        )
        r.joined[:, at] = (value + bias).astype(bf16)

    seg_row = r.seg_row[...].astype(f32)
    r.seg_col[...] = jnp.broadcast_to(seg_row, (8, rows)).T[:, :1]
    for i in range(rows // B):
        at, ends = slice(i * B, (i + 1) * B), (i + 1) * B
        here = lax.broadcasted_iota(jnp.int32, (B, ends), 0) + i * B
        there = lax.broadcasted_iota(jnp.int32, (B, ends), 1)
        allowed = (r.seg_col[at, :] == seg_row[:, :ends]) & (there <= here)
        r.part_m[at, :ends] = jnp.where(allowed, (there - here).astype(f32), -1e34)
    pl.semaphore_wait(barrier, 9)
    loads["cot"].wait()
    start_block(COT, r.cot)
    start_block(FI, r.first_in)

    for h in range(heads):
        start = 3 * h * HD
        power = (seat * heads + h + 1).astype(f32) * (-8.0 / H)
        slope = jnp.exp2(jnp.full((1, rows), power, f32))
        for i in range(rows // B):
            at, ends = slice(i * B, (i + 1) * B), (i + 1) * B
            raw = contract(
                r.joined[at, start : start + HD], r.joined[:ends, start + HD : start + 2 * HD], 1, 1
            )
            scores = raw * scaling + slope[:, :ends] * r.part_m[at, :ends]
            weights = jnp.exp(scores - jnp.max(scores, axis=-1, keepdims=True))
            prob = weights * (1.0 / jnp.sum(weights, axis=-1, keepdims=True))
            r.probs[h, at, :ends] = prob
            if ends < rows:
                r.probs[h, at, ends:] = jnp.zeros((B, rows - ends), f32)
            value = contract(
                prob.astype(bf16), r.joined[:ends, start + 2 * HD : start + 3 * HD], 1, 0
            ).astype(bf16)
            r.ctx_b[at, h * HD : (h + 1) * HD] = value
    r.ctx_s[...] = r.ctx_b[...].astype(f32)
    ctx_send().start()
    loads["w_dense_v"].wait()
    make_partial(ATT, lambda at, n: contract(r.ctx_b[at, :], r.w_dense_v[:, rows_at(n, W)], 1, 0))
    open_sum(ATT)

    loads["w_down_v"].wait()

    def early(k):
        at = rows_at(k, W)
        r.broad[:, at] = contract(r.cot[...], r.w_down_v[at, :], 1, 1)

    loop(n_u, early)
    loop(rows // 16, lambda i: gather(BDOWN, r.cot[rows_at(i, 16), :].astype(f32)))
    pass_block(COT)
    pass_block(FI)
    for t in range(4):
        r.right[:rows, t * B : (t + 1) * B] = r.cot[:, column(t, x)]
        r.left_q[t * B : (t + 1) * B, :rows] = (
            r.first_in[:, column(t, x)].astype(f32).T.astype(bf16)
        )
    def second_norm(start):
        def body(i):
            at = pl.ds(pl.multiple_of(start + i * 16, 16), 16)
            values = r.tok[at, :].astype(f32) + r.sum_a[at, :] + r.bias_dense[...]
            average = jnp.mean(values, axis=-1, keepdims=True)
            centered = values - average
            inverse = lax.rsqrt(jnp.mean(centered * centered, axis=-1, keepdims=True) + EPSILON)
            r.hidden[at, :] = values
            r.average2[at, :] = average
            r.inverse2[at, :] = inverse
            r.second_in[at, :] = (centered * inverse * r.gain2[...] + r.shift2[...]).astype(bf16)

        loop(sub // 16, body)

    close_all(ATT, second_norm)

    loads["w_up_v"].wait()
    for j, (kind, k, lo, size) in enumerate(items):
        if kind != "down":
            continue
        part, columns = slice(lo, lo + size), slice(k * W + lo, k * W + lo + size)
        r.act_s[k, :, part] = (
            contract(r.second_in[...], r.w_up_v[:, columns], 1, 0) + r.bias_up[:, columns]
        )

        def gelu_step(i, k=k, part=part, columns=columns):
            at = rows_at(i, 32)
            value, slope = gelu_pair(r.act_s[k, at, part])
            r.act_s[k, at, part] = value
            r.act_b[k, at, part] = value.astype(bf16)
            change = r.broad[at, columns] * slope
            r.gu_s[k, at, part] = change
            r.gu_b[k, at, part] = change.astype(bf16)
            gather(BUP, change, columns)

        loop(rows // 32, gelu_step)
        x_send(j).start()
    blk_send(COT).wait_send()
    start_block(SI, r.second_in)
    start_items("up", range(n_u))

    def up_terms(at, n):
        return sum(
            contract(r.gu_b[k, at, :], r.w_up_v[rows_at(n, W), k * W : (k + 1) * W], 1, 1)
            for k in range(n_u)
        )

    def mixed_terms(at, n):
        return sum(
            contract(r.act_b[k, at, :], r.w_down_v[k * W : (k + 1) * W, rows_at(n, W)], 1, 0)
            for k in range(n_u)
        )

    take_block(COT)
    for t in range(4):
        r.right[rows:, t * B : (t + 1) * B] = r.blk_r[COT, t].astype(bf16)
    advance(0)
    for k in range(CHUNKS):
        near_copy(ATT, k).wait_send()
    make_partial(GN2, up_terms)
    for k in range(CHUNKS):
        back_copy(ATT, k).wait_send()
    open_sum(GN2)
    advance(1)
    for t in range(4):
        r.left_u[t * B : (t + 1) * B, :rows] = (
            r.second_in[:, column(t, x)].astype(f32).T.astype(bf16)
        )
    take_block(FI)
    for t in range(4):
        r.left_q[t * B : (t + 1) * B, rows:] = r.blk_r[FI, t].T.astype(bf16)
    advance(2)
    advance(3)

    def hidden_step(start):
        def body(i):
            at = pl.ds(pl.multiple_of(start + i * 16, 16), 16)
            upstream = r.sum_a[at, :]
            normed = (r.hidden[at, :] - r.average2[at, :]) * r.inverse2[at, :]
            change = norm_backward(upstream, normed, r.inverse2[at, :], r.gain2[...])
            value = r.cot[at, :].astype(f32) + change
            r.broad[at, :] = value
            r.gh_b[at, :] = value.astype(bf16)
            gather(GAIN2, upstream * normed)
            gather(SHIFT2, upstream)
            gather(BDENSE, value)

        loop(sub // 16, body)

    close_all(GN2, hidden_step)
    blk_send(FI).wait_send()
    start_block(GH, r.gh_b)
    r.gctx[...] = contract(r.gh_b[...], r.w_dense_v[...], 1, 1).astype(bf16)
    advance(4)

    for h in range(heads):
        start = 3 * h * HD
        queries = r.joined[:, start : start + HD]
        key_vecs = r.joined[:, start + HD : start + 2 * HD]
        val_vecs = r.joined[:, start + 2 * HD : start + 3 * HD]
        upstream = r.gctx[:, h * HD : (h + 1) * HD]
        prob = r.probs[h]
        grad_probs = contract(upstream, val_vecs, 1, 1)
        row_inner = jnp.sum(prob * grad_probs, axis=-1, keepdims=True)
        grad_scores = (prob * (grad_probs - row_inner)).astype(bf16)
        thirds = (
            contract(grad_scores, key_vecs, 1, 0) * scaling,
            contract(grad_scores, queries, 0, 0) * scaling,
            contract(prob.astype(bf16), upstream, 0, 0),
        )
        for third, value in enumerate(thirds):
            k, offset = divmod(start + third * HD, W)
            r.gj_s[k, :, offset : offset + HD] = value
    for k in range(n_q):
        start_items("qkv", (k,))

        def joined_grad(i, k=k):
            at = rows_at(i, 32)
            value = r.gj_s[k, at, :]
            r.gj_b[k, at, :] = value.astype(bf16)
            gather(BQKV, value, slice(k * W, (k + 1) * W))

        loop(rows // 32, joined_grad)

    def joined_terms(at, n):
        return sum(
            contract(r.gj_b[k, at, :], r.w_qkv_v[rows_at(n, W), k * W : (k + 1) * W], 1, 1)
            for k in range(n_q)
        )

    for k in range(CHUNKS):
        near_copy(GN2, k).wait_send()
        back_copy(GN2, k).wait_send()
    make_partial(GN1, joined_terms)
    pass_block(SI)
    open_sum(GN1)
    take_block(SI)
    for t in range(4):
        r.left_u[t * B : (t + 1) * B, rows:] = r.blk_r[SI, t].T.astype(bf16)

    advance(5)
    make_partial(MIX, mixed_terms)
    open_sum(MIX)
    advance(6)

    def input_step(start):
        def body(i):
            at = pl.ds(pl.multiple_of(start + i * 16, 16), 16)
            upstream = r.sum_a[at, :]
            inverse = r.inverse1[at, :]
            normed = (r.tok[at, :].astype(f32) - r.average1[at, :]) * inverse
            change = norm_backward(upstream, normed, inverse, r.gain1[...])
            gather(GAIN1, upstream * normed)
            gather(SHIFT1, upstream)
            r.broad[at, :] = r.broad[at, :] + change

        loop(sub // 16, body)

    close_all(GN1, input_step)
    input_copy = pltpu.make_async_copy(r.broad, r.grad_input, r.load_sem.at[1])
    input_copy.start()

    for v in range(8):
        vector = jnp.sum(r.acc[v], axis=0, keepdims=True)
        if v == BQKV:
            piece = n_q * W // 8
        else:
            piece = B
        for p in range(8):
            r.table[p, v : v + 1, :piece] = vector[:, p * piece : (p + 1) * piece]

    def vector_send(step):
        peer = (place + step) % 8
        return send(
            r.table.at[peer], r.vec_r.at[step], r.vs.at[step], r.vr.at[step], {"dp": peer}
        )

    for step in range(1, 8):
        vector_send(step).start()
    advance(7)

    advance(8)
    pass_block(GH)
    for t in range(4):
        r.right[:rows, t * B : (t + 1) * B] = r.gh_b[:, column(t, x)]
    take_block(GH)
    for t in range(4):
        r.right[rows:, t * B : (t + 1) * B] = r.blk_r[GH, t].astype(bf16)
    ctx_send().wait_recv()
    advance(9)
    vector = r.table[place]
    for step in range(1, 8):
        vector_send(step).wait_recv()
        vector = vector + r.vec_r[step]
    r.vectors[...] = vector
    advance(10)
    def output_step(start):
        def body(i):
            at = pl.ds(pl.multiple_of(start + i * 16, 16), 16)
            value = r.hidden[at, :] + r.sum_m[at, :] + r.bias_down[...]
            r.second_in[at, :] = value.astype(bf16)

        loop(sub // 16, body)

    close_all(MIX, output_step)
    output_copy = pltpu.make_async_copy(r.second_in, r.output, r.load_sem.at[0])
    output_copy.start()
    advance(11)

    for j in range(12, len(items) + FINISH):
        advance(j)

    for j, item in enumerate(items):
        if item[0] != "dense":
            x_send(j).wait_send()
    ctx_send().wait_send()
    for n in range(4):
        if n in (SI, GH):
            blk_send(n).wait_send()
        for i in range(3):
            blk_pass(n, i).wait_send()
    for a in range(SUMS):
        for k in range(CHUNKS):
            if a in (MIX, GN1):
                near_copy(a, k).wait_send()
                back_copy(a, k).wait_send()
            far_copy(a, k).wait_send()
    for step in range(1, 8):
        vector_send(step).wait_send()
    for j in range(len(items)):
        for t in range(4):

            @pl.when(z < t)
            def _():
                up(j, t).wait_send()

            @pl.when(z > t)
            def _():
                down(j, t, False).wait_send()

        result_copy(j).wait()
    output_copy.wait()
    input_copy.wait()


def deliver_kernel(count, *refs):
    sources, vectors = refs[:count], refs[count]
    results, lines = refs[count + 1 : 2 * count + 1], refs[2 * count + 1 : 2 * count + 9]
    held, table = refs[2 * count + 9 : 3 * count + 9], refs[3 * count + 9]
    parts, load_sem, store_sem = refs[3 * count + 10 : -2], refs[-2], refs[-1]
    loads = [
        pltpu.make_async_copy(src, mid, load_sem.at[i])
        for i, (src, mid) in enumerate(zip((vectors, *sources), (table, *held)))
    ]
    stores = [
        pltpu.make_async_copy(mid, dst, store_sem.at[i])
        for i, (mid, dst) in enumerate(zip((*held, *parts), (*results, *lines)))
    ]
    for copy in loads:
        copy.start()
    loads[0].wait()
    for v, part in enumerate(parts):
        part[...] = table[v : v + 1, : part.shape[1]]
        stores[count + v].start()
    for load, store in zip(loads[1:], stores):
        load.wait()
        store.start()
    for store in stores:
        store.wait()


def whole_layer(tokens, segment_ids, cotangent, *rest):
    (
        norm1_gain,
        norm1_shift,
        w_qkv,
        b_qkv,
        w_dense,
        b_dense,
        norm2_gain,
        norm2_shift,
        w_up,
        b_up,
        w_down,
        b_down,
    ) = rest
    rows, width = tokens.shape
    joined = w_qkv.shape[1]
    heads = joined // (3 * HD)
    inner = heads * HD
    units = w_up.shape[1]
    n_u, n_q = units // W, joined // W
    n_wide = n_u + n_q
    items = [("down", 0, 0, B), ("down", 0, B, B)]
    items += [("down", k, 0, W) for k in range(1, n_u)]
    items += [("up", k, 0, W) for k in range(n_u)] + [("dense", 0, 0, W)]
    items += [("qkv", k, 0, W) for k in range(n_q - 1)]
    items += [("qkv", n_q - 1, 0, B), ("qkv", n_q - 1, B, B)]
    n_all = len(items)
    sub = rows // 2 // CHUNKS
    inputs = [
        ("seg_row", segment_ids),
        ("gain1", norm1_gain[None]),
        ("shift1", norm1_shift[None]),
        ("bias_qkv", b_qkv.reshape(-1, B)),
        ("bias_dense", b_dense[None]),
        ("gain2", norm2_gain[None]),
        ("shift2", norm2_shift[None]),
        ("bias_up", b_up[None]),
        ("bias_down", b_down[None]),
        ("tokens", tokens),
        ("cotangent", cotangent),
        ("w_qkv", w_qkv),
        ("w_dense", w_dense),
        ("w_up", w_up),
        ("w_down", w_down),
    ]
    small = 9
    outs = [
        ("output", (rows, width), bf16),
        ("grad_input", (rows, width), f32),
        ("grad_w_qkv", (width // 8, joined), f32),
        ("grad_w_dense", (inner, width // 8), f32),
        ("grad_w_up", (width // 8, units), f32),
        ("grad_w_down", (units, width // 8), f32),
        ("vectors", (8, B), f32),
    ]
    dma = pltpu.SemaphoreType.DMA
    scratch = [
        ("tok", (rows, width), bf16),
        ("cot", (rows, width), bf16),
        ("w_qkv_v", w_qkv.shape, bf16),
        ("w_dense_v", w_dense.shape, bf16),
        ("w_up_v", w_up.shape, bf16),
        ("w_down_v", w_down.shape, bf16),
        ("seg_col", (rows, 1), f32),
        ("average1", (rows, 1), f32),
        ("inverse1", (rows, 1), f32),
        ("average2", (rows, 1), f32),
        ("inverse2", (rows, 1), f32),
        ("first_in", (rows, width), bf16),
        ("second_in", (rows, width), bf16),
        ("hidden", (rows, width), f32),
        ("broad", (rows, width), f32),
        ("gh_b", (rows, width), bf16),
        ("joined", (rows, joined), bf16),
        ("probs", (heads, rows, rows), f32),
        ("ctx_b", (rows, inner), bf16),
        ("gctx", (rows, inner), bf16),
        ("act_b", (n_u, rows, W), bf16),
        ("gu_b", (n_u, rows, W), bf16),
        ("gj_b", (n_q, rows, W), bf16),
        ("act_s", (n_u, rows, W), f32),
        ("act_r", (n_u, rows, W), f32),
        ("gu_s", (n_u, rows, W), f32),
        ("gu_r", (n_u, rows, W), f32),
        ("gj_s", (n_q, rows, W), f32),
        ("gj_r", (n_q, rows, W), f32),
        ("ctx_s", (rows, inner), f32),
        ("ctx_r", (rows, inner), f32),
        ("blk_s", (2, rows, B), f32),
        ("blk_r", (4, 4, rows, B), f32),
        ("right", (2 * rows, 4 * B), bf16),
        ("left_u", (4 * B, 2 * rows), bf16),
        ("left_q", (4 * B, 2 * rows), bf16),
        ("part_a", (rows, width), f32),
        ("part_m", (rows, width), f32),
        ("sum_a", (rows, width), f32),
        ("sum_m", (rows, width), f32),
        ("near", (SUMS, CHUNKS, sub, width), f32),
        ("far", (SUMS, CHUNKS, sub, width), f32),
        ("own_t", (N_TALL, 4, W, B), f32),
        ("in_t", (N_TALL, 4, W, B), f32),
        ("end_t", (N_TALL, W, B), f32),
        ("own_w", (n_wide, 4, B, W), f32),
        ("in_w", (n_wide, 4, B, W), f32),
        ("end_w", (n_wide, B, W), f32),
        ("acc", (8, 8, width), f32),
        ("table", (8, 8, B), f32),
        ("vec_r", (8, 8, B), f32),
    ]
    sems = [
        ("load_sem", (6,)),
        ("out_sem", (n_all,)),
        ("xs", (n_all,)),
        ("xr", (n_all,)),
        ("ctx_ss", None),
        ("ctx_rs", None),
        ("bs", (4,)),
        ("br", (4,)),
        ("fs", (4, 3)),
        ("fr", (4, 3)),
        ("cs", (SUMS, CHUNKS)),
        ("cr", (SUMS, CHUNKS)),
        ("ys", (SUMS, CHUNKS)),
        ("yr", (SUMS, CHUNKS)),
        ("ks", (SUMS, CHUNKS)),
        ("kr", (SUMS, CHUNKS)),
        ("us", (n_all, 4)),
        ("ur", (n_all, 4)),
        ("ds", (n_all, 4)),
        ("dr", (n_all, 4)),
        ("vs", (8,)),
        ("vr", (8,)),
    ]
    names = [n for n, _ in inputs] + [o[0] for o in outs] + [s[0] for s in scratch]
    names += [n for n, _ in sems]
    vmem, anywhere = pl.BlockSpec(memory_space=pltpu.VMEM), pl.BlockSpec(memory_space=pl.ANY)
    results = pl.pallas_call(
        functools.partial(layer_kernel, names, items),
        out_shape=[jax.ShapeDtypeStruct(shape, kind) for _, shape, kind in outs],
        in_specs=[vmem] * small + [anywhere] * (len(inputs) - small),
        out_specs=[anywhere] * (len(outs) - 1) + [vmem],
        scratch_shapes=[pltpu.VMEM(shape, kind) for _, shape, kind in scratch]
        + [dma(shape) if shape else dma for _, shape in sems],
        compiler_params=pltpu.CompilerParams(
            collective_id=7, has_side_effects=True, vmem_limit_bytes=63 * MIB
        ),
    )(*[value for _, value in inputs])
    lengths = [joined // 8 if v == BQKV else B for v in range(8)]
    results = pl.pallas_call(
        functools.partial(deliver_kernel, len(outs) - 1),
        out_shape=[jax.ShapeDtypeStruct(o.shape, o.dtype) for o in results[:-1]]
        + [jax.ShapeDtypeStruct((1, n), f32) for n in lengths],
        in_specs=[anywhere] * len(outs),
        out_specs=[anywhere] * (len(outs) + 7),
        scratch_shapes=[pltpu.VMEM(o.shape, o.dtype) for o in results]
        + [pltpu.VMEM((1, n), f32) for n in lengths]
        + [dma((len(outs),)), dma((len(outs) + 7,))],
    )(*results)
    output, grad_input, g_qkv, g_dense, g_up, g_down = results[: len(outs) - 1]
    v = [o.reshape(-1) for o in results[len(outs) - 1 :]]
    return (
        output,
        grad_input,
        v[GAIN1],
        v[SHIFT1],
        g_qkv,
        v[BQKV],
        g_dense,
        v[BDENSE],
        v[GAIN2],
        v[SHIFT2],
        g_up,
        v[BUP],
        g_down,
        v[BDOWN],
    )


def solution(mesh):
    in_specs = (
        P("dp", None),
        P("dp", None),
        P("dp", None),
        P(),
        P(),
        P(None, "tensor"),
        P("tensor"),
        P("tensor", None),
        P(),
        P(),
        P(),
        P(None, "tensor"),
        P("tensor"),
        P("tensor", None),
        P(),
    )
    out_specs = (
        P("dp", None),
        P("dp", None),
        P("dp"),
        P("dp"),
        P("dp", "tensor"),
        P(("tensor", "dp")),
        P("tensor", "dp"),
        P("dp"),
        P("dp"),
        P("dp"),
        P("dp", "tensor"),
        P(("tensor", "dp")),
        P("tensor", "dp"),
        P("dp"),
    )
    sizes = (mesh.shape["dp"], mesh.shape["tensor"])
    body = whole_layer if sizes == (8, 4) else functools.partial(local, sizes)
    return jax.shard_map(body, mesh=mesh, in_specs=in_specs, out_specs=out_specs, check_vma=False)
```

```python
import functools
import math
from types import SimpleNamespace

import jax
import jax.numpy as jnp
from jax import lax
from jax.experimental import pallas as pl
from jax.experimental.pallas import tpu as pltpu
from jax.sharding import PartitionSpec as P

H = 16
HD = 64


EPSILON = 1e-05
GELU_COEF = math.sqrt(2.0 / math.pi)


def layer_norm(values, gain, shift):
    average = jnp.mean(values, axis=-1, keepdims=True)
    centered = values - average
    variance = jnp.mean(centered * centered, axis=-1, keepdims=True)
    inverse = lax.rsqrt(variance + EPSILON)
    normed = centered * inverse
    return (normed * gain + shift, normed, inverse)


def norm_backward(upstream, normed, inverse, gain):
    scaled = upstream * gain
    return inverse * (
        scaled
        - jnp.mean(scaled, axis=-1, keepdims=True)
        - normed * jnp.mean(scaled * normed, axis=-1, keepdims=True)
    )


def gelu_pair(inputs):
    tangent = jnp.tanh(GELU_COEF * (inputs + 0.044715 * inputs * inputs * inputs))
    result = 0.5 * inputs * (1.0 + tangent)
    derivative = 0.5 * (1.0 + tangent) + 0.5 * inputs * (1.0 - tangent * tangent) * GELU_COEF * (
        1.0 + 3.0 * 0.044715 * inputs * inputs
    )
    return (result, derivative)


def head_scores(queries, key_vecs, slopes, offset, allowed, scaling):
    raw_scores = jnp.einsum("ihe,jhe->hij", queries, key_vecs, preferred_element_type=jnp.float32)
    return jnp.where(
        allowed[None], raw_scores * scaling + slopes[:, None, None] * offset[None], -1e30
    )

CHUNKS = 4
MESH = pl.DeviceIdType.MESH
MIB = 1024 * 1024


def scatter(grads, kinds):
    return [
        lax.psum_scatter(g, "dp", scatter_dimension=0 if k == "rows" else 1, tiled=True)
        for g, k in zip(grads, kinds)
    ]


def scatter_vectors(vectors, n_dp):
    widths = [v.shape[0] // n_dp for v in vectors]
    widest = -(-max(widths) // 128) * 128
    table = jnp.stack(
        [jnp.pad(v.reshape(n_dp, -1), ((0, 0), (0, widest - w))) for v, w in zip(vectors, widths)],
        axis=1,
    ).reshape(n_dp * len(vectors), widest)
    (mine,) = scatter([table], ["rows"])
    return [mine[i, :w] for i, w in enumerate(widths)]


def local(
    sizes,
    tokens,
    segment_ids,
    cotangent,
    norm1_gain,
    norm1_shift,
    w_qkv,
    b_qkv,
    w_dense,
    b_dense,
    norm2_gain,
    norm2_shift,
    w_up,
    b_up,
    w_down,
    b_down,
):
    segments = segment_ids[0]
    row_count = tokens.shape[0]
    heads_here = w_qkv.shape[1] // (3 * HD)
    head_start = lax.axis_index("tensor") * heads_here
    scaling = 1.0 / math.sqrt(HD)
    slopes = 2.0 ** (-8.0 * (head_start + jnp.arange(heads_here) + 1).astype(jnp.float32) / H)
    places = jnp.arange(row_count)
    offset = (places[None, :] - places[:, None]).astype(jnp.float32)
    allowed = (segments[:, None] == segments[None, :]) & (places[None, :] <= places[:, None])
    inputs = tokens.astype(jnp.float32)
    first_out, normed1, inverse1 = layer_norm(inputs, norm1_gain, norm1_shift)
    first_in = first_out.astype(jnp.bfloat16)
    joined = (jnp.dot(first_in, w_qkv, preferred_element_type=jnp.float32) + b_qkv).astype(
        jnp.bfloat16
    )
    joined = joined.reshape(row_count, heads_here, 3, HD)
    queries = joined[:, :, 0]
    key_vecs = joined[:, :, 1]
    val_vecs = joined[:, :, 2]
    scores = head_scores(queries, key_vecs, slopes, offset, allowed, scaling)
    highest = jnp.max(scores, axis=-1, keepdims=True)
    log_total = highest + jnp.log(jnp.sum(jnp.exp(scores - highest), axis=-1, keepdims=True))
    probs = jnp.exp(scores - log_total)
    probs_b = probs.astype(jnp.bfloat16)
    context = jnp.einsum(
        "hij,jhe->ihe", probs_b, val_vecs, preferred_element_type=jnp.float32
    ).astype(jnp.bfloat16)
    context = context.reshape(row_count, heads_here * HD)
    attended = lax.psum(jnp.dot(context, w_dense, preferred_element_type=jnp.float32), "tensor")
    hidden = inputs + attended + b_dense
    second_out, normed2, inverse2 = layer_norm(hidden, norm2_gain, norm2_shift)
    second_in = second_out.astype(jnp.bfloat16)
    upward = jnp.dot(second_in, w_up, preferred_element_type=jnp.float32) + b_up
    activated, gelu_slope = gelu_pair(upward)
    activated_b = activated.astype(jnp.bfloat16)
    mixed = jnp.dot(activated_b, w_down, preferred_element_type=jnp.float32)
    grad_out = cotangent.astype(jnp.float32)
    grad_w_down = jnp.dot(activated_b.T, cotangent, preferred_element_type=jnp.float32)
    grad_b_down = jnp.sum(grad_out, axis=0)
    grad_up = jnp.dot(cotangent, w_down.T, preferred_element_type=jnp.float32) * gelu_slope
    grad_up_b = grad_up.astype(jnp.bfloat16)
    grad_w_up = jnp.dot(second_in.T, grad_up_b, preferred_element_type=jnp.float32)
    grad_b_up = jnp.sum(grad_up, axis=0)
    grad_norm2 = jnp.dot(grad_up_b, w_up.T, preferred_element_type=jnp.float32)
    grad_norm2 = lax.psum(grad_norm2, "tensor")
    mixed = lax.psum(mixed, "tensor")
    grad_hidden = grad_out + norm_backward(grad_norm2, normed2, inverse2, norm2_gain)
    grad_hidden_b = grad_hidden.astype(jnp.bfloat16)
    grad_w_dense = jnp.dot(context.T, grad_hidden_b, preferred_element_type=jnp.float32)
    grad_context = jnp.dot(grad_hidden_b, w_dense.T, preferred_element_type=jnp.float32).astype(
        jnp.bfloat16
    )
    grad_context = grad_context.reshape(row_count, heads_here, HD)
    scores_again = head_scores(queries, key_vecs, slopes, offset, allowed, scaling)
    probs_again = jnp.exp(scores_again - log_total)
    probs_again_b = probs_again.astype(jnp.bfloat16)
    grad_vals = jnp.einsum(
        "hij,ihe->jhe", probs_again_b, grad_context, preferred_element_type=jnp.float32
    )
    grad_probs = jnp.einsum(
        "ihe,jhe->hij", grad_context, val_vecs, preferred_element_type=jnp.float32
    )
    row_inner = jnp.sum(probs_again * grad_probs, axis=-1, keepdims=True)
    grad_scores = (probs_again * (grad_probs - row_inner)).astype(jnp.bfloat16)
    grad_queries = (
        jnp.einsum("hij,jhe->ihe", grad_scores, key_vecs, preferred_element_type=jnp.float32)
        * scaling
    )
    grad_keys = (
        jnp.einsum("hij,ihe->jhe", grad_scores, queries, preferred_element_type=jnp.float32)
        * scaling
    )
    grad_joined = jnp.stack([grad_queries, grad_keys, grad_vals], axis=2).reshape(
        row_count, 3 * heads_here * HD
    )
    grad_joined_b = grad_joined.astype(jnp.bfloat16)
    grad_w_qkv = jnp.dot(first_in.T, grad_joined_b, preferred_element_type=jnp.float32)
    grad_norm1 = jnp.dot(grad_joined_b, w_qkv.T, preferred_element_type=jnp.float32)
    grad_norm1 = lax.psum(grad_norm1, "tensor")
    grad_w_up, grad_w_down, grad_w_qkv, grad_w_dense = scatter(
        [grad_w_up, grad_w_down, grad_w_qkv, grad_w_dense],
        ["rows", "columns", "rows", "columns"],
    )
    output = (hidden + mixed + b_down).astype(jnp.bfloat16)
    grad_gain2 = jnp.sum(grad_norm2 * normed2, axis=0)
    grad_shift2 = jnp.sum(grad_norm2, axis=0)
    grad_b_dense = jnp.sum(grad_hidden, axis=0)
    grad_b_qkv = jnp.sum(grad_joined, axis=0)
    grad_gain1 = jnp.sum(grad_norm1 * normed1, axis=0)
    grad_shift1 = jnp.sum(grad_norm1, axis=0)
    grad_input = grad_hidden + norm_backward(grad_norm1, normed1, inverse1, norm1_gain)
    vectors = scatter_vectors(
        [
            grad_gain1,
            grad_shift1,
            grad_b_qkv,
            grad_b_dense,
            grad_gain2,
            grad_shift2,
            grad_b_up,
            grad_b_down,
        ],
        sizes[0],
    )
    gain1, shift1, b_qkv_part, b_dense_part, gain2, shift2, b_up_part, b_down_part = vectors
    return (
        output,
        grad_input,
        gain1,
        shift1,
        grad_w_qkv,
        b_qkv_part,
        grad_w_dense,
        b_dense_part,
        gain2,
        shift2,
        grad_w_up,
        b_up_part,
        grad_w_down,
        b_down_part,
    )


W = 256
B = 128
SUMS = 4
ATT, GN2, MIX, GN1 = range(SUMS)
COT, FI, SI, GH = range(4)
GAIN1, SHIFT1, BQKV, BDENSE, GAIN2, SHIFT2, BUP, BDOWN = range(8)
N_TALL = 5
RELAY, AGAIN, FINISH = 1, 2, 4
f32 = jnp.float32
bf16 = jnp.bfloat16


def contract(left, right, left_axis, right_axis):
    return lax.dot_general(
        left, right, (((left_axis,), (right_axis,)), ((), ())), preferred_element_type=f32
    )


def loop(count, body):
    def step(i, carry):
        body(i)
        return carry

    lax.fori_loop(0, count, step, 0)


def rows_at(i, size):
    return pl.ds(pl.multiple_of(i * size, size), size)


def layer_kernel(names, items, *refs):
    r = SimpleNamespace(**dict(zip(names, refs)))
    rows, width = r.tok.shape
    half = rows // 2
    sub = half // CHUNKS
    heads = r.probs.shape[0]
    units = r.w_up_v.shape[1]
    n_u = units // W
    n_q = r.w_qkv_v.shape[1] // W
    scaling = 1.0 / math.sqrt(HD)
    place, seat = lax.axis_index("dp"), lax.axis_index("tensor")
    z, x = place // 2, place % 2
    y, core = seat // 2, seat % 2
    other_x = {"dp": z * 2 + 1 - x}
    above, below = {"dp": place + 2}, {"dp": place - 2}
    other_core = {"tensor": y * 2 + 1 - core}
    other_y = {"tensor": (1 - y) * 2 + core}

    loads = {}
    pairs = [
        ("tok", "tokens"),
        ("w_qkv_v", "w_qkv"),
        ("cot", "cotangent"),
        ("w_dense_v", "w_dense"),
        ("w_down_v", "w_down"),
        ("w_up_v", "w_up"),
    ]
    for i, (dst, src) in enumerate(pairs):
        loads[dst] = pltpu.make_async_copy(getattr(r, src), getattr(r, dst), r.load_sem.at[i])
        loads[dst].start()

    barrier = pltpu.get_barrier_semaphore()
    for step in range(1, 8):
        peer = {"dp": (place + step) % 8}
        pl.semaphore_signal(barrier, inc=1, device_id=peer, device_id_type=MESH)
    pl.semaphore_signal(barrier, inc=1, device_id=other_core, device_id_type=MESH)
    pl.semaphore_signal(barrier, inc=1, device_id=other_y, device_id_type=MESH)

    def send(src, dst, send_sem, recv_sem, device):
        return pltpu.make_async_remote_copy(
            src_ref=src,
            dst_ref=dst,
            send_sem=send_sem,
            recv_sem=recv_sem,
            device_id=device,
            device_id_type=MESH,
        )

    def x_send(j):
        kind, k, lo, size = items[j]
        out, into = {"down": (r.act_s, r.act_r), "up": (r.gu_s, r.gu_r), "qkv": (r.gj_s, r.gj_r)}[
            kind
        ]
        at = (k, slice(None), pl.ds(lo, size))
        return send(out.at[at], into.at[at], r.xs.at[j], r.xr.at[j], other_x)

    def start_items(kind, ks):
        for j, item in enumerate(items):
            if item[0] == kind and item[1] in ks:
                x_send(j).start()

    def ctx_send():
        return send(r.ctx_s, r.ctx_r, r.ctx_ss, r.ctx_rs, other_x)

    def blk_send(n):
        return send(r.blk_s.at[n % 2], r.blk_r.at[n, seat], r.bs.at[n], r.br.at[n], other_x)

    def blk_pass(n, i):
        part = r.blk_r.at[n, (seat if i < 2 else 2 * (1 - y) + core)]
        device = other_y if i == 1 else other_core
        return send(part, part, r.fs.at[n, i], r.fr.at[n, i], device)

    def column(t, side):
        return pl.ds(pl.multiple_of((2 * t + side) * B, B), B)

    def start_block(n, source):
        r.blk_s[n % 2] = source[:, column(seat, 1 - x)].astype(f32)
        blk_send(n).start()

    def pass_block(n):
        blk_send(n).wait_recv()
        blk_pass(n, 0).start()
        blk_pass(n, 1).start()

    def take_block(n):
        blk_pass(n, 1).wait_recv()
        blk_pass(n, 2).start()
        blk_pass(n, 0).wait_recv()
        blk_pass(n, 2).wait_recv()

    def partial(a):
        return r.part_m if a == MIX else r.part_a

    def total(a):
        return r.sum_m if a == MIX else r.sum_a

    def own(k):
        return pl.ds(pl.multiple_of(core * half + k * sub, sub), sub)

    def its(k):
        return pl.ds(pl.multiple_of((1 - core) * half + k * sub, sub), sub)

    def near_copy(a, k):
        return send(
            partial(a).at[its(k), :], r.near.at[a, k], r.cs.at[a, k], r.cr.at[a, k], other_core
        )

    def far_copy(a, k):
        return send(r.near.at[a, k], r.far.at[a, k], r.ys.at[a, k], r.yr.at[a, k], other_y)

    def back_copy(a, k):
        part = total(a).at[own(k), :]
        return send(part, part, r.ks.at[a, k], r.kr.at[a, k], other_core)

    def make_partial(a, terms):
        dst = partial(a)
        for side in (1, 0):
            start = pl.multiple_of((core if side == 0 else 1 - core) * half, half)
            at = pl.ds(start, half)
            loop(width // W, lambda n: dst.__setitem__((at, rows_at(n, W)), terms(at, n)))
            if side:
                for k in range(CHUNKS):
                    near_copy(a, k).start()

    def open_sum(a):
        for k in range(CHUNKS):
            near_copy(a, k).wait_recv()
            r.near[a, k] = r.near[a, k] + partial(a)[own(k), :]
            far_copy(a, k).start()

    def close_sum(a, k):
        far_copy(a, k).wait_recv()
        total(a)[own(k), :] = r.near[a, k] + r.far[a, k]
        back_copy(a, k).start()

    def close_all(a, work):
        for k in range(CHUNKS):
            close_sum(a, k)
            work(core * half + k * sub)
            if k:
                back_copy(a, k - 1).wait_recv()
                work((1 - core) * half + (k - 1) * sub)
        back_copy(a, CHUNKS - 1).wait_recv()
        work((1 - core) * half + (CHUNKS - 1) * sub)

    def gather(v, values, at=None):
        part = values[0:8]
        for i in range(1, values.shape[0] // 8):
            part = part + values[8 * i : 8 * i + 8]
        if at is None:
            r.acc[v] = r.acc[v] + part
        else:
            r.acc[v, :, at] = r.acc[v, :, at] + part

    slots, n_tall, n_wide = [], 0, 0
    for kind, _, lo, size in items:
        if kind in ("down", "dense"):
            slots.append((r.own_t, r.in_t, r.end_t, n_tall))
            n_tall += lo + size == W
        else:
            slots.append((r.own_w, r.in_w, r.end_w, n_wide))
            n_wide += lo + size == W

    def view(ref, j, *at):
        kind, _, lo, size = items[j]
        rest = (pl.ds(lo, size),) if kind in ("down", "dense") else (slice(None), pl.ds(lo, size))
        return ref.at[(slots[j][3], *at, *rest)]

    def up(j, t):
        mine, into, _, _ = slots[j]
        return send(view(mine, j, t), view(into, j, t), r.us.at[j, t], r.ur.at[j, t], above)

    def down(j, t, last):
        mine, into, end, _ = slots[j]
        dst = view(end, j) if last else view(into, j, t)
        return send(view(mine, j, t), dst, r.ds.at[j, t], r.dr.at[j, t], below)

    def product(j):
        kind, k, lo, size = items[j]
        mine = slots[j][0]
        at = slice(lo, lo + size)
        if kind != "dense":
            x_send(j).wait_recv()
        if kind == "down":
            value = contract(r.act_b[k, :, at], r.right[:rows], 0, 0) + contract(
                r.act_r[k, :, at].astype(bf16), r.right[rows:], 0, 0
            )
        elif kind == "dense":
            value = contract(r.ctx_b[...], r.right[:rows], 0, 0) + contract(
                r.ctx_r[...].astype(bf16), r.right[rows:], 0, 0
            )
        else:
            if kind == "up":
                left, here, there = r.left_u, r.gu_b[k, :, at], r.gu_r[k, :, at]
            else:
                left, here, there = r.left_q, r.gj_b[k, :, at], r.gj_r[k, :, at]
            value = contract(left[:, :rows], here, 1, 0) + contract(
                left[:, rows:], there.astype(bf16), 1, 0
            )
        for t in range(4):
            part = slice(t * B, (t + 1) * B)
            view(mine, j, t)[...] = value[:, part] if kind in ("down", "dense") else value[part]

        @pl.when(z == 0)
        def _():
            for t in (3, 2, 1):
                up(j, t).start()

        @pl.when(z == 3)
        def _():
            for t in (0, 1, 2):
                down(j, t, t == 2).start()

    def pass_on(j, t, here, upward):
        mine, into, _, _ = slots[j]

        @pl.when(z == here)
        def _():
            came = up(j, t) if upward else down(j, t, False)
            came.wait_recv()
            view(mine, j, t)[...] = view(mine, j, t)[...] + view(into, j, t)[...]
            onward = up(j, t) if upward else down(j, t, t == here - 1)
            onward.start()

    def relay(j):
        pass_on(j, 3, 1, True)
        pass_on(j, 2, 1, True)
        pass_on(j, 0, 2, False)
        pass_on(j, 1, 2, False)

    def relay_again(j):
        pass_on(j, 3, 2, True)
        pass_on(j, 0, 1, False)

    def result_copy(j):
        kind, k, lo, size = items[j]
        out = getattr(r, "grad_w_" + kind)
        at = pl.ds(k * W + lo, size)
        dst = out.at[at, :] if kind in ("down", "dense") else out.at[:, at]
        return pltpu.make_async_copy(view(slots[j][0], j, z), dst, r.out_sem.at[j])

    def finish(j):
        mine, into, end, _ = slots[j]

        @pl.when(z > 0)
        def _():
            up(j, z).wait_recv()
            view(mine, j, z)[...] = view(mine, j, z)[...] + view(into, j, z)[...]

        @pl.when(z < 3)
        def _():
            down(j, z, True).wait_recv()
            view(mine, j, z)[...] = view(mine, j, z)[...] + view(end, j)[...]

        result_copy(j).start()

    def advance(j):
        if j < len(items):
            product(j)
        for lag, step in ((RELAY, relay), (AGAIN, relay_again), (FINISH, finish)):
            if 0 <= j - lag < len(items):
                step(j - lag)

    r.acc[...] = jnp.zeros_like(r.acc)
    loads["tok"].wait()

    def first_norm(i):
        at = rows_at(i, 32)
        values = r.tok[at, :].astype(f32)
        average = jnp.mean(values, axis=-1, keepdims=True)
        centered = values - average
        inverse = lax.rsqrt(jnp.mean(centered * centered, axis=-1, keepdims=True) + EPSILON)
        r.average1[at, :] = average
        r.inverse1[at, :] = inverse
        r.first_in[at, :] = (centered * inverse * r.gain1[...] + r.shift1[...]).astype(bf16)

    loop(rows // 32, first_norm)
    loads["w_qkv_v"].wait()

    for n in range(n_q):
        at = slice(n * W, (n + 1) * W)
        value = contract(r.first_in[...], r.w_qkv_v[:, at], 1, 0)
        bias = jnp.concatenate(
            [r.bias_qkv[i : i + 1] for i in range(n * W // B, (n + 1) * W // B)], axis=1
        )
        r.joined[:, at] = (value + bias).astype(bf16)

    seg_row = r.seg_row[...].astype(f32)
    r.seg_col[...] = jnp.broadcast_to(seg_row, (8, rows)).T[:, :1]
    for i in range(rows // B):
        at, ends = slice(i * B, (i + 1) * B), (i + 1) * B
        here = lax.broadcasted_iota(jnp.int32, (B, ends), 0) + i * B
        there = lax.broadcasted_iota(jnp.int32, (B, ends), 1)
        allowed = (r.seg_col[at, :] == seg_row[:, :ends]) & (there <= here)
        r.part_m[at, :ends] = jnp.where(allowed, (there - here).astype(f32), -1e34)
    pl.semaphore_wait(barrier, 9)
    loads["cot"].wait()
    start_block(COT, r.cot)
    start_block(FI, r.first_in)

    for h in range(heads):
        start = 3 * h * HD
        power = (seat * heads + h + 1).astype(f32) * (-8.0 / H)
        slope = jnp.exp2(jnp.full((1, rows), power, f32))
        for i in range(rows // B):
            at, ends = slice(i * B, (i + 1) * B), (i + 1) * B
            raw = contract(
                r.joined[at, start : start + HD], r.joined[:ends, start + HD : start + 2 * HD], 1, 1
            )
            scores = raw * scaling + slope[:, :ends] * r.part_m[at, :ends]
            weights = jnp.exp(scores - jnp.max(scores, axis=-1, keepdims=True))
            prob = weights * (1.0 / jnp.sum(weights, axis=-1, keepdims=True))
            r.probs[h, at, :ends] = prob
            if ends < rows:
                r.probs[h, at, ends:] = jnp.zeros((B, rows - ends), f32)
            value = contract(
                prob.astype(bf16), r.joined[:ends, start + 2 * HD : start + 3 * HD], 1, 0
            ).astype(bf16)
            r.ctx_b[at, h * HD : (h + 1) * HD] = value
    r.ctx_s[...] = r.ctx_b[...].astype(f32)
    ctx_send().start()
    loads["w_dense_v"].wait()
    make_partial(ATT, lambda at, n: contract(r.ctx_b[at, :], r.w_dense_v[:, rows_at(n, W)], 1, 0))
    open_sum(ATT)

    loads["w_down_v"].wait()

    def early(k):
        at = rows_at(k, W)
        r.broad[:, at] = contract(r.cot[...], r.w_down_v[at, :], 1, 1)

    loop(n_u, early)
    loop(rows // 16, lambda i: gather(BDOWN, r.cot[rows_at(i, 16), :].astype(f32)))
    pass_block(COT)
    pass_block(FI)
    for t in range(4):
        r.right[:rows, t * B : (t + 1) * B] = r.cot[:, column(t, x)]
        r.left_q[t * B : (t + 1) * B, :rows] = (
            r.first_in[:, column(t, x)].astype(f32).T.astype(bf16)
        )
    def second_norm(start):
        def body(i):
            at = pl.ds(pl.multiple_of(start + i * 16, 16), 16)
            values = r.tok[at, :].astype(f32) + r.sum_a[at, :] + r.bias_dense[...]
            average = jnp.mean(values, axis=-1, keepdims=True)
            centered = values - average
            inverse = lax.rsqrt(jnp.mean(centered * centered, axis=-1, keepdims=True) + EPSILON)
            r.hidden[at, :] = values
            r.average2[at, :] = average
            r.inverse2[at, :] = inverse
            r.second_in[at, :] = (centered * inverse * r.gain2[...] + r.shift2[...]).astype(bf16)

        loop(sub // 16, body)

    close_all(ATT, second_norm)

    loads["w_up_v"].wait()
    blk_send(COT).wait_send()
    start_block(SI, r.second_in)
    for j, (kind, k, lo, size) in enumerate(items):
        if kind != "down":
            continue
        part, columns = slice(lo, lo + size), slice(k * W + lo, k * W + lo + size)
        r.act_s[k, :, part] = (
            contract(r.second_in[...], r.w_up_v[:, columns], 1, 0) + r.bias_up[:, columns]
        )

        def gelu_step(i, k=k, part=part, columns=columns):
            at = rows_at(i, 32)
            value, slope = gelu_pair(r.act_s[k, at, part])
            r.act_s[k, at, part] = value
            r.act_b[k, at, part] = value.astype(bf16)
            change = r.broad[at, columns] * slope
            r.gu_s[k, at, part] = change
            r.gu_b[k, at, part] = change.astype(bf16)
            gather(BUP, change, columns)

        loop(rows // 32, gelu_step)
        x_send(j).start()
    start_items("up", range(n_u))

    def up_terms(at, n):
        return sum(
            contract(r.gu_b[k, at, :], r.w_up_v[rows_at(n, W), k * W : (k + 1) * W], 1, 1)
            for k in range(n_u)
        )

    def mixed_terms(at, n):
        return sum(
            contract(r.act_b[k, at, :], r.w_down_v[k * W : (k + 1) * W, rows_at(n, W)], 1, 0)
            for k in range(n_u)
        )

    take_block(COT)
    for t in range(4):
        r.right[rows:, t * B : (t + 1) * B] = r.blk_r[COT, t].astype(bf16)
    pass_block(SI)
    advance(0)
    for k in range(CHUNKS):
        near_copy(ATT, k).wait_send()
    make_partial(GN2, up_terms)
    for k in range(CHUNKS):
        back_copy(ATT, k).wait_send()
    open_sum(GN2)
    advance(1)
    for t in range(4):
        r.left_u[t * B : (t + 1) * B, :rows] = (
            r.second_in[:, column(t, x)].astype(f32).T.astype(bf16)
        )
    take_block(FI)
    for t in range(4):
        r.left_q[t * B : (t + 1) * B, rows:] = r.blk_r[FI, t].T.astype(bf16)
    advance(2)
    advance(3)

    def hidden_step(start):
        def body(i):
            at = pl.ds(pl.multiple_of(start + i * 16, 16), 16)
            upstream = r.sum_a[at, :]
            normed = (r.hidden[at, :] - r.average2[at, :]) * r.inverse2[at, :]
            change = norm_backward(upstream, normed, r.inverse2[at, :], r.gain2[...])
            value = r.cot[at, :].astype(f32) + change
            r.broad[at, :] = value
            r.gh_b[at, :] = value.astype(bf16)
            gather(GAIN2, upstream * normed)
            gather(SHIFT2, upstream)
            gather(BDENSE, value)

        loop(sub // 16, body)

    close_all(GN2, hidden_step)
    blk_send(FI).wait_send()
    start_block(GH, r.gh_b)
    r.gctx[...] = contract(r.gh_b[...], r.w_dense_v[...], 1, 1).astype(bf16)
    advance(4)

    for h in range(heads):
        start = 3 * h * HD
        queries = r.joined[:, start : start + HD]
        key_vecs = r.joined[:, start + HD : start + 2 * HD]
        val_vecs = r.joined[:, start + 2 * HD : start + 3 * HD]
        upstream = r.gctx[:, h * HD : (h + 1) * HD]
        prob = r.probs[h]
        grad_probs = contract(upstream, val_vecs, 1, 1)
        row_inner = jnp.sum(prob * grad_probs, axis=-1, keepdims=True)
        grad_scores = (prob * (grad_probs - row_inner)).astype(bf16)
        thirds = (
            contract(grad_scores, key_vecs, 1, 0) * scaling,
            contract(grad_scores, queries, 0, 0) * scaling,
            contract(prob.astype(bf16), upstream, 0, 0),
        )
        for third, value in enumerate(thirds):
            k, offset = divmod(start + third * HD, W)
            r.gj_s[k, :, offset : offset + HD] = value
    for k in range(n_q):
        start_items("qkv", (k,))

        def joined_grad(i, k=k):
            at = rows_at(i, 32)
            value = r.gj_s[k, at, :]
            r.gj_b[k, at, :] = value.astype(bf16)
            gather(BQKV, value, slice(k * W, (k + 1) * W))

        loop(rows // 32, joined_grad)

    def joined_terms(at, n):
        return sum(
            contract(r.gj_b[k, at, :], r.w_qkv_v[rows_at(n, W), k * W : (k + 1) * W], 1, 1)
            for k in range(n_q)
        )

    for k in range(CHUNKS):
        near_copy(GN2, k).wait_send()
        back_copy(GN2, k).wait_send()
    make_partial(GN1, joined_terms)
    open_sum(GN1)
    take_block(SI)
    for t in range(4):
        r.left_u[t * B : (t + 1) * B, rows:] = r.blk_r[SI, t].T.astype(bf16)

    advance(5)
    make_partial(MIX, mixed_terms)
    open_sum(MIX)
    advance(6)

    def input_step(start):
        def body(i):
            at = pl.ds(pl.multiple_of(start + i * 16, 16), 16)
            upstream = r.sum_a[at, :]
            inverse = r.inverse1[at, :]
            normed = (r.tok[at, :].astype(f32) - r.average1[at, :]) * inverse
            change = norm_backward(upstream, normed, inverse, r.gain1[...])
            gather(GAIN1, upstream * normed)
            gather(SHIFT1, upstream)
            r.broad[at, :] = r.broad[at, :] + change

        loop(sub // 16, body)

    close_all(GN1, input_step)
    input_copy = pltpu.make_async_copy(r.broad, r.grad_input, r.load_sem.at[1])
    input_copy.start()

    for v in range(8):
        vector = jnp.sum(r.acc[v], axis=0, keepdims=True)
        if v == BQKV:
            piece = n_q * W // 8
        else:
            piece = B
        for p in range(8):
            r.table[p, v : v + 1, :piece] = vector[:, p * piece : (p + 1) * piece]

    def vector_send(step):
        peer = (place + step) % 8
        return send(
            r.table.at[peer], r.vec_r.at[step], r.vs.at[step], r.vr.at[step], {"dp": peer}
        )

    for step in range(1, 8):
        vector_send(step).start()
    advance(7)

    advance(8)
    pass_block(GH)
    for t in range(4):
        r.right[:rows, t * B : (t + 1) * B] = r.gh_b[:, column(t, x)]
    take_block(GH)
    for t in range(4):
        r.right[rows:, t * B : (t + 1) * B] = r.blk_r[GH, t].astype(bf16)
    ctx_send().wait_recv()
    advance(9)
    vector = r.table[place]
    for step in range(1, 8):
        vector_send(step).wait_recv()
        vector = vector + r.vec_r[step]
    r.vectors[...] = vector
    advance(10)
    def output_step(start):
        def body(i):
            at = pl.ds(pl.multiple_of(start + i * 16, 16), 16)
            value = r.hidden[at, :] + r.sum_m[at, :] + r.bias_down[...]
            r.second_in[at, :] = value.astype(bf16)

        loop(sub // 16, body)

    close_all(MIX, output_step)
    output_copy = pltpu.make_async_copy(r.second_in, r.output, r.load_sem.at[0])
    output_copy.start()
    advance(11)

    for j in range(12, len(items) + FINISH):
        advance(j)

    for j, item in enumerate(items):
        if item[0] != "dense":
            x_send(j).wait_send()
    ctx_send().wait_send()
    for n in range(4):
        if n in (SI, GH):
            blk_send(n).wait_send()
        for i in range(3):
            blk_pass(n, i).wait_send()
    for a in range(SUMS):
        for k in range(CHUNKS):
            if a in (MIX, GN1):
                near_copy(a, k).wait_send()
                back_copy(a, k).wait_send()
            far_copy(a, k).wait_send()
    for step in range(1, 8):
        vector_send(step).wait_send()
    for j in range(len(items)):
        for t in range(4):

            @pl.when(z < t)
            def _():
                up(j, t).wait_send()

            @pl.when(z > t)
            def _():
                down(j, t, False).wait_send()

        result_copy(j).wait()
    output_copy.wait()
    input_copy.wait()


def deliver_kernel(count, *refs):
    sources, vectors = refs[:count], refs[count]
    results, lines = refs[count + 1 : 2 * count + 1], refs[2 * count + 1 : 2 * count + 9]
    held, table = refs[2 * count + 9 : 3 * count + 9], refs[3 * count + 9]
    parts, load_sem, store_sem = refs[3 * count + 10 : -2], refs[-2], refs[-1]
    loads = [
        pltpu.make_async_copy(src, mid, load_sem.at[i])
        for i, (src, mid) in enumerate(zip((vectors, *sources), (table, *held)))
    ]
    stores = [
        pltpu.make_async_copy(mid, dst, store_sem.at[i])
        for i, (mid, dst) in enumerate(zip((*held, *parts), (*results, *lines)))
    ]
    for copy in loads:
        copy.start()
    loads[0].wait()
    for v, part in enumerate(parts):
        part[...] = table[v : v + 1, : part.shape[1]]
        stores[count + v].start()
    for load, store in zip(loads[1:], stores):
        load.wait()
        store.start()
    for store in stores:
        store.wait()


def whole_layer(tokens, segment_ids, cotangent, *rest):
    (
        norm1_gain,
        norm1_shift,
        w_qkv,
        b_qkv,
        w_dense,
        b_dense,
        norm2_gain,
        norm2_shift,
        w_up,
        b_up,
        w_down,
        b_down,
    ) = rest
    rows, width = tokens.shape
    joined = w_qkv.shape[1]
    heads = joined // (3 * HD)
    inner = heads * HD
    units = w_up.shape[1]
    n_u, n_q = units // W, joined // W
    n_wide = n_u + n_q
    items = [("down", 0, 0, B), ("down", 0, B, B)]
    items += [("down", k, 0, W) for k in range(1, n_u)]
    items += [("up", k, 0, W) for k in range(n_u)] + [("dense", 0, 0, W)]
    items += [("qkv", k, 0, W) for k in range(n_q - 1)]
    items += [("qkv", n_q - 1, 0, B), ("qkv", n_q - 1, B, B)]
    n_all = len(items)
    sub = rows // 2 // CHUNKS
    inputs = [
        ("seg_row", segment_ids),
        ("gain1", norm1_gain[None]),
        ("shift1", norm1_shift[None]),
        ("bias_qkv", b_qkv.reshape(-1, B)),
        ("bias_dense", b_dense[None]),
        ("gain2", norm2_gain[None]),
        ("shift2", norm2_shift[None]),
        ("bias_up", b_up[None]),
        ("bias_down", b_down[None]),
        ("tokens", tokens),
        ("cotangent", cotangent),
        ("w_qkv", w_qkv),
        ("w_dense", w_dense),
        ("w_up", w_up),
        ("w_down", w_down),
    ]
    small = 9
    outs = [
        ("output", (rows, width), bf16),
        ("grad_input", (rows, width), f32),
        ("grad_w_qkv", (width // 8, joined), f32),
        ("grad_w_dense", (inner, width // 8), f32),
        ("grad_w_up", (width // 8, units), f32),
        ("grad_w_down", (units, width // 8), f32),
        ("vectors", (8, B), f32),
    ]
    dma = pltpu.SemaphoreType.DMA
    scratch = [
        ("tok", (rows, width), bf16),
        ("cot", (rows, width), bf16),
        ("w_qkv_v", w_qkv.shape, bf16),
        ("w_dense_v", w_dense.shape, bf16),
        ("w_up_v", w_up.shape, bf16),
        ("w_down_v", w_down.shape, bf16),
        ("seg_col", (rows, 1), f32),
        ("average1", (rows, 1), f32),
        ("inverse1", (rows, 1), f32),
        ("average2", (rows, 1), f32),
        ("inverse2", (rows, 1), f32),
        ("first_in", (rows, width), bf16),
        ("second_in", (rows, width), bf16),
        ("hidden", (rows, width), f32),
        ("broad", (rows, width), f32),
        ("gh_b", (rows, width), bf16),
        ("joined", (rows, joined), bf16),
        ("probs", (heads, rows, rows), f32),
        ("ctx_b", (rows, inner), bf16),
        ("gctx", (rows, inner), bf16),
        ("act_b", (n_u, rows, W), bf16),
        ("gu_b", (n_u, rows, W), bf16),
        ("gj_b", (n_q, rows, W), bf16),
        ("act_s", (n_u, rows, W), f32),
        ("act_r", (n_u, rows, W), f32),
        ("gu_s", (n_u, rows, W), f32),
        ("gu_r", (n_u, rows, W), f32),
        ("gj_s", (n_q, rows, W), f32),
        ("gj_r", (n_q, rows, W), f32),
        ("ctx_s", (rows, inner), f32),
        ("ctx_r", (rows, inner), f32),
        ("blk_s", (2, rows, B), f32),
        ("blk_r", (4, 4, rows, B), f32),
        ("right", (2 * rows, 4 * B), bf16),
        ("left_u", (4 * B, 2 * rows), bf16),
        ("left_q", (4 * B, 2 * rows), bf16),
        ("part_a", (rows, width), f32),
        ("part_m", (rows, width), f32),
        ("sum_a", (rows, width), f32),
        ("sum_m", (rows, width), f32),
        ("near", (SUMS, CHUNKS, sub, width), f32),
        ("far", (SUMS, CHUNKS, sub, width), f32),
        ("own_t", (N_TALL, 4, W, B), f32),
        ("in_t", (N_TALL, 4, W, B), f32),
        ("end_t", (N_TALL, W, B), f32),
        ("own_w", (n_wide, 4, B, W), f32),
        ("in_w", (n_wide, 4, B, W), f32),
        ("end_w", (n_wide, B, W), f32),
        ("acc", (8, 8, width), f32),
        ("table", (8, 8, B), f32),
        ("vec_r", (8, 8, B), f32),
    ]
    sems = [
        ("load_sem", (6,)),
        ("out_sem", (n_all,)),
        ("xs", (n_all,)),
        ("xr", (n_all,)),
        ("ctx_ss", None),
        ("ctx_rs", None),
        ("bs", (4,)),
        ("br", (4,)),
        ("fs", (4, 3)),
        ("fr", (4, 3)),
        ("cs", (SUMS, CHUNKS)),
        ("cr", (SUMS, CHUNKS)),
        ("ys", (SUMS, CHUNKS)),
        ("yr", (SUMS, CHUNKS)),
        ("ks", (SUMS, CHUNKS)),
        ("kr", (SUMS, CHUNKS)),
        ("us", (n_all, 4)),
        ("ur", (n_all, 4)),
        ("ds", (n_all, 4)),
        ("dr", (n_all, 4)),
        ("vs", (8,)),
        ("vr", (8,)),
    ]
    names = [n for n, _ in inputs] + [o[0] for o in outs] + [s[0] for s in scratch]
    names += [n for n, _ in sems]
    vmem, anywhere = pl.BlockSpec(memory_space=pltpu.VMEM), pl.BlockSpec(memory_space=pl.ANY)
    results = pl.pallas_call(
        functools.partial(layer_kernel, names, items),
        out_shape=[jax.ShapeDtypeStruct(shape, kind) for _, shape, kind in outs],
        in_specs=[vmem] * small + [anywhere] * (len(inputs) - small),
        out_specs=[anywhere] * (len(outs) - 1) + [vmem],
        scratch_shapes=[pltpu.VMEM(shape, kind) for _, shape, kind in scratch]
        + [dma(shape) if shape else dma for _, shape in sems],
        compiler_params=pltpu.CompilerParams(
            collective_id=7, has_side_effects=True, vmem_limit_bytes=63 * MIB
        ),
    )(*[value for _, value in inputs])
    lengths = [joined // 8 if v == BQKV else B for v in range(8)]
    results = pl.pallas_call(
        functools.partial(deliver_kernel, len(outs) - 1),
        out_shape=[jax.ShapeDtypeStruct(o.shape, o.dtype) for o in results[:-1]]
        + [jax.ShapeDtypeStruct((1, n), f32) for n in lengths],
        in_specs=[anywhere] * len(outs),
        out_specs=[anywhere] * (len(outs) + 7),
        scratch_shapes=[pltpu.VMEM(o.shape, o.dtype) for o in results]
        + [pltpu.VMEM((1, n), f32) for n in lengths]
        + [dma((len(outs),)), dma((len(outs) + 7,))],
    )(*results)
    output, grad_input, g_qkv, g_dense, g_up, g_down = results[: len(outs) - 1]
    v = [o.reshape(-1) for o in results[len(outs) - 1 :]]
    return (
        output,
        grad_input,
        v[GAIN1],
        v[SHIFT1],
        g_qkv,
        v[BQKV],
        g_dense,
        v[BDENSE],
        v[GAIN2],
        v[SHIFT2],
        g_up,
        v[BUP],
        g_down,
        v[BDOWN],
    )


def solution(mesh):
    in_specs = (
        P("dp", None),
        P("dp", None),
        P("dp", None),
        P(),
        P(),
        P(None, "tensor"),
        P("tensor"),
        P("tensor", None),
        P(),
        P(),
        P(),
        P(None, "tensor"),
        P("tensor"),
        P("tensor", None),
        P(),
    )
    out_specs = (
        P("dp", None),
        P("dp", None),
        P("dp"),
        P("dp"),
        P("dp", "tensor"),
        P(("tensor", "dp")),
        P("tensor", "dp"),
        P("dp"),
        P("dp"),
        P("dp"),
        P("dp", "tensor"),
        P(("tensor", "dp")),
        P("tensor", "dp"),
        P("dp"),
    )
    sizes = (mesh.shape["dp"], mesh.shape["tensor"])
    body = whole_layer if sizes == (8, 4) else functools.partial(local, sizes)
    return jax.shard_map(body, mesh=mesh, in_specs=in_specs, out_specs=out_specs, check_vma=False)
```
